256 devices in a mesh: dp: 32 (over z, y), seq: 8 (over x, core).
Axes of the slice: x: 4, y: 4, z: 8, core: 2. Of those that a mesh axis runs over, the one named last changes fastest.
Arguments:
- slot_tokens: bfloat16 [416, 512, 1152], P('dp', 'seq'), may hold values from -12 to 12
- modulation: float32 [32, 6, 1152], P('dp'), may hold values from -2.5 to 2.5
- counts: int32 [32], replicated, may hold values from 1 to 13, as said below
- dest: int32 [32, 13], replicated, may hold values from 0 to 223, as said below
- qkv_spatial: bfloat16 [1152, 1728], replicated, may hold values from -4 to 4
- out_spatial: bfloat16 [576, 1152], replicated, may hold values from -0.25 to 0.25
- qkv_temporal: bfloat16 [1152, 1728], replicated, may hold values from -4 to 4
- out_temporal: bfloat16 [576, 1152], replicated, may hold values from -0.25 to 0.25
Outputs:
- video_out: bfloat16 [224, 512, 1152], P('dp', 'seq')
The draws below stay inside these ranges and needn't reach their ends.
Inputs may be any that keep to these rules, and one draw needn't show every extreme that they name: Group g holds blocks in slots 0 to counts[g] - 1; the counts sum to 224; some group holds 13 blocks. Over the slots q below counts[g] of all groups g, dest[g, q] takes every value 0 to 223 exactly once; one group sends at most 1 block to one video, and some group sends 1; entries at slots from counts[g] on are arbitrary values of the same range.
All inputs are finite; a program needn't handle non-finite values.
Results may differ from the reference program's by a relative error of at most 0.0057.
Values may be sent and summed in bfloat16 or wider, within the bound.
No kernel may reach another device: no remote copies, remote signals or barrier semaphores. Data moves between devices by JAX's collectives and lax.ppermute only.
A program may use at most 64 MiB of HBM per device.

```python
import math
import jax
import jax.numpy as jnp
from jax import lax

D = 1152
HEADS = 8
HEAD_DIM = 72
PATCHES = 64
NFD = 7
HD = 576
SLOTS = 13
PMAX = 8
N_DP = 32
N_SEQ = 8


def route_plan(base_key):
    group_count = N_DP
    plan_key = jax.random.fold_in(base_key, 404)
    pair_order = jax.random.permutation(jax.random.fold_in(plan_key, 1), group_count)
    changes = jax.random.randint(jax.random.fold_in(plan_key, 2), (group_count // 2,), 0, NFD)
    changes = changes.at[0].set(SLOTS - NFD).astype(jnp.int32)
    counts = jnp.full((group_count,), NFD, jnp.int32)
    counts = counts.at[pair_order[0::2]].add(changes).at[pair_order[1::2]].add(-changes)
    order = jax.random.permutation(jax.random.fold_in(plan_key, 3), group_count)
    ordered = counts[order]
    offsets_ordered = jnp.cumsum(ordered).astype(jnp.int32) - ordered
    offsets = jnp.zeros((group_count,), jnp.int32).at[order].set(offsets_ordered)
    video_order = jax.random.permutation(jax.random.fold_in(plan_key, 4), group_count).astype(jnp.int32)
    rotations = jax.random.randint(jax.random.fold_in(plan_key, 5), (group_count,), 0, NFD)
    slot_ids = jnp.arange(SLOTS, dtype=jnp.int32)
    items = offsets[:, None] + slot_ids[None, :]
    videos = video_order[items % group_count]
    positions = (items // group_count + rotations[videos]) % NFD
    live_dest = videos * NFD + positions
    filler = jax.random.randint(jax.random.fold_in(plan_key, 6), (group_count, SLOTS), 0, group_count * NFD)
    dest = jnp.where(slot_ids[None, :] < counts[:, None], live_dest, filler)
    return (counts.astype(jnp.int32), dest.astype(jnp.int32))


def draw_counts(key, part):
    return route_plan(key)[0]


def draw_dest(key, part):
    return route_plan(key)[1]


def draw_slot_tokens(key, part):
    token_key = jax.random.fold_in(key, 303)
    rows = N_DP * SLOTS
    columns = N_SEQ * PATCHES
    base = jax.random.normal(jax.random.fold_in(token_key, 1), (rows, columns, D), jnp.float32)
    row_scale = jnp.exp(jax.random.uniform(jax.random.fold_in(token_key, 3), (rows, columns, 1), jnp.float32, math.log(0.3), math.log(3.0)))
    column_scale = jnp.exp(jax.random.uniform(jax.random.fold_in(token_key, 4), (D,), jnp.float32, math.log(0.5), math.log(2.0)))
    return jnp.clip(base * row_scale * column_scale, -12.0, 12.0).astype(jnp.bfloat16)


def projection_draw(weight_key):
    entries = jax.random.normal(jax.random.fold_in(weight_key, 1), (D, 3, HEADS, HEAD_DIM), jnp.float32) / math.sqrt(D)
    return jnp.clip(entries.reshape(D, 3 * HEADS * HEAD_DIM), -4.0, 4.0).astype(jnp.bfloat16)


def draw_qkv_spatial(key, part):
    return projection_draw(jax.random.fold_in(key, 101))


def draw_qkv_temporal(key, part):
    return projection_draw(jax.random.fold_in(key, 202))


def block_levels(key, shape, cuts, smallest, largest):
    gain, own = 1.0, jax.random.fold_in(key, 6)
    for dim, shards_of in cuts:
        steps = jnp.exp(jax.random.uniform(jax.random.fold_in(own, dim), (shards_of,), jnp.float32, smallest / len(cuts), largest / len(cuts)))
        gain = gain * jnp.repeat(steps, shape[dim] // shards_of).reshape([-1 if axis == dim else 1 for axis in range(len(shape))])
    return gain


def gaussian(stream_key, shape, width, reach, shards=(), kind=jnp.bfloat16):
    drawn = width * jax.random.normal(stream_key, shape, jnp.float32)
    if shards:
        drawn = drawn * block_levels(stream_key, shape, shards, -0.22, 0.18)
    return jnp.clip(drawn, -reach, reach).astype(kind)


def setup_inputs(seed: int = 0) -> dict:
    splits = jax.random.split(jax.random.key(seed), 9)
    slot_tokens = draw_slot_tokens(jax.random.fold_in(splits[8], 71), 0)
    modulation = gaussian(splits[1], (N_DP, 6, D), 0.5, 2.5, ((0, 32),), jnp.float32)
    counts = draw_counts(jax.random.fold_in(splits[8], 71), 0)
    dest = draw_dest(jax.random.fold_in(splits[8], 71), 0)
    qkv_spatial = draw_qkv_spatial(jax.random.fold_in(splits[8], 71), 0)
    out_spatial = gaussian(splits[5], (HD, D), HD ** -0.5, 0.25)
    qkv_temporal = draw_qkv_temporal(jax.random.fold_in(splits[8], 71), 0)
    out_temporal = gaussian(splits[7], (HD, D), HD ** -0.5, 0.25)
    return dict(slot_tokens=slot_tokens, modulation=modulation, counts=counts, dest=dest, qkv_spatial=qkv_spatial, out_spatial=out_spatial, qkv_temporal=qkv_temporal, out_temporal=out_temporal)


epsilon = 1e-06

def norm_mod(tokens, shift_row, scale_row):
    values = tokens.astype(jnp.float32)
    center = values - lax.optimization_barrier(jnp.mean(values, axis=-1, keepdims=True))
    spread = lax.optimization_barrier(jnp.mean(center * center, axis=-1, keepdims=True))
    return (center * lax.rsqrt(spread + epsilon) * (1.0 + scale_row) + shift_row).astype(jnp.bfloat16)

def attend(qkv_rows, batch_count, length):
    parts = qkv_rows.astype(jnp.float32).reshape(batch_count, length, 3, HEADS, HEAD_DIM)
    factor = 1.0 / math.sqrt(HEAD_DIM)
    scores = jnp.einsum('bqhs,bkhs->bhqk', parts[:, :, 0], parts[:, :, 1]) * factor
    highest = lax.optimization_barrier(jnp.max(scores, axis=-1, keepdims=True))
    raised = jnp.exp(scores - highest)
    weights = (raised / lax.optimization_barrier(jnp.sum(raised, axis=-1, keepdims=True))).astype(jnp.bfloat16)
    mixed = jnp.einsum('bhqk,bkhs->bqhs', weights.astype(jnp.float32), parts[:, :, 2])
    return mixed.astype(jnp.bfloat16).reshape(batch_count * length, HEADS * HEAD_DIM)

def reference(slot_tokens, modulation, counts, dest, qkv_spatial, out_spatial, qkv_temporal, out_temporal):
    slot_ids = jnp.arange(SLOTS, dtype=jnp.int32)
    live_slots = slot_ids[None, :] < counts[:, None]
    targets = jnp.where(live_slots, dest, N_DP * NFD).astype(jnp.int32).reshape(-1)
    anchors = (jnp.arange(N_DP, dtype=jnp.int32)[:, None] * SLOTS + slot_ids[None, :]).astype(jnp.int32).reshape(-1)
    source_of = jnp.zeros((N_DP * NFD,), jnp.int32).at[targets].set(anchors, mode='drop')
    video_blocks = jnp.take(slot_tokens, source_of, axis=0)
    videos = video_blocks.reshape(N_DP, NFD * N_SEQ, PATCHES, D)

    def one_video(pair):
        video_frames, video_modulation = pair
        frame_count = video_frames.shape[0]
        normed = norm_mod(video_frames, video_modulation[0], video_modulation[1])
        qkv_rows = jnp.dot(normed.reshape(-1, D), qkv_spatial, preferred_element_type=jnp.float32).astype(jnp.bfloat16)
        mixed = attend(qkv_rows, frame_count, PATCHES)
        projected = jnp.dot(mixed, out_spatial, preferred_element_type=jnp.float32).reshape(frame_count, PATCHES, D)
        after_spatial = (video_frames.astype(jnp.float32) + video_modulation[2] * projected).astype(jnp.bfloat16)
        grouped = after_spatial.reshape(frame_count, N_SEQ, PMAX, D)
        grouped = grouped.transpose(1, 0, 2, 3).reshape(N_SEQ, frame_count * PMAX, D)
        normed_two = norm_mod(grouped, video_modulation[3], video_modulation[4])
        qkv_two = jnp.dot(normed_two.reshape(-1, D), qkv_temporal, preferred_element_type=jnp.float32).astype(jnp.bfloat16)
        qkv_two = qkv_two.reshape(N_SEQ, frame_count, PMAX, 3 * HD).transpose(0, 2, 1, 3).reshape(N_SEQ * PMAX * frame_count, 3 * HD)
        mixed_two = attend(qkv_two, N_SEQ * PMAX, frame_count)
        mixed_two = mixed_two.reshape(N_SEQ, PMAX, frame_count, HD).transpose(0, 2, 1, 3).reshape(N_SEQ * frame_count * PMAX, HD)
        projected_two = jnp.dot(mixed_two, out_temporal, preferred_element_type=jnp.float32).reshape(N_SEQ, frame_count * PMAX, D)
        result = (grouped.astype(jnp.float32) + video_modulation[5] * projected_two).astype(jnp.bfloat16)
        return result.reshape(N_SEQ, frame_count, PMAX, D).transpose(1, 0, 2, 3).reshape(frame_count, PATCHES, D)
    outputs = lax.map(one_video, (videos, modulation))
    return outputs.reshape(N_DP * NFD, N_SEQ * PATCHES, D)
```

```python
import math

import jax
import jax.numpy as jnp
from jax import lax
from jax.sharding import PartitionSpec as P

HEADS = 8
HEAD_DIM = 72
NFD = 7
EPS = 1e-06


def norm_mod(tokens, shift_row, scale_row):
    values = tokens.astype(jnp.float32)
    center = values - jnp.mean(values, axis=-1, keepdims=True)
    spread = jnp.mean(center * center, axis=-1, keepdims=True)
    return (center * lax.rsqrt(spread + EPS) * (1.0 + scale_row) + shift_row).astype(jnp.bfloat16)


def attention(qkv_rows, batch_count, length):
    parts = qkv_rows.reshape(batch_count, length, 3, HEADS, HEAD_DIM)
    factor = 1.0 / math.sqrt(HEAD_DIM)
    scores = (
        jnp.einsum("bqhs,bkhs->bhqk", parts[:, :, 0], parts[:, :, 1], preferred_element_type=jnp.float32)
        * factor
    )
    highest = jnp.max(scores, axis=-1, keepdims=True)
    raised = jnp.exp(scores - highest)
    weights = (raised / jnp.sum(raised, axis=-1, keepdims=True)).astype(jnp.bfloat16)
    mixed = jnp.einsum("bhqk,bkhs->bqhs", weights, parts[:, :, 2], preferred_element_type=jnp.float32)
    return mixed.astype(jnp.bfloat16).reshape(batch_count * length, HEADS * HEAD_DIM)


def block(rows, shift, scale, gate, w_qkv, w_out, attend):
    normed = norm_mod(rows, shift, scale)
    qkv = jnp.dot(normed, w_qkv, preferred_element_type=jnp.float32).astype(jnp.bfloat16)
    mixed = attend(qkv)
    projected = jnp.dot(mixed, w_out, preferred_element_type=jnp.float32)
    return (rows.astype(jnp.float32) + gate * projected).astype(jnp.bfloat16)


def source_index(counts, dest):
    groups, slots = dest.shape
    slot_ids = jnp.arange(slots, dtype=jnp.int32)
    live = slot_ids[None, :] < counts[:, None]
    targets = jnp.where(live, dest, -1).reshape(-1)
    wanted = jnp.arange(groups * NFD, dtype=jnp.int32)
    anchors = jnp.arange(groups * slots, dtype=jnp.int32)
    return jnp.sum(jnp.where(targets[None, :] == wanted[:, None], anchors[None, :], 0), axis=1)


def on_device(slot_tokens, modulation, counts, dest, qkv_spatial, out_spatial, qkv_temporal, out_temporal):
    groups = lax.axis_size("dp")
    shards = lax.axis_size("seq")
    slots, patches, width = slot_tokens.shape
    piece = patches // groups
    mod = modulation[0]
    pieces = slot_tokens.reshape(slots, groups, piece, width).transpose(1, 0, 2, 3)
    spread = lax.all_to_all(pieces, "dp", split_axis=0, concat_axis=0, tiled=True)
    chosen = jnp.take(spread.reshape(groups * slots, piece, width), source_index(counts, dest), axis=0)
    gathered = lax.all_to_all(
        chosen.reshape(groups, NFD, piece, width), "dp", split_axis=0, concat_axis=0, tiled=True
    )
    frames = gathered.transpose(1, 0, 2, 3).reshape(NFD * patches, width)
    after = block(
        frames, mod[0], mod[1], mod[2], qkv_spatial, out_spatial, lambda qkv: attention(qkv, NFD, patches)
    )
    widest = patches // shards
    total = shards * NFD
    moved = lax.all_to_all(
        after.reshape(NFD, shards, widest, width), "seq", split_axis=1, concat_axis=0, tiled=True
    )

    def attend(qkv):
        by_patch = qkv.reshape(total, widest, -1).transpose(1, 0, 2).reshape(widest * total, -1)
        mixed = attention(by_patch, widest, total)
        return mixed.reshape(widest, total, -1).transpose(1, 0, 2).reshape(total * widest, -1)

    home = block(
        moved.reshape(total * widest, width), mod[3], mod[4], mod[5], qkv_temporal, out_temporal, attend
    )
    back = lax.all_to_all(
        home.reshape(total, 1, widest, width), "seq", split_axis=0, concat_axis=1, tiled=True
    )
    return back.reshape(NFD, patches, width)


def solution(mesh):
    in_specs = (P("dp", "seq", None), P("dp", None, None), P(), P(), P(), P(), P(), P())
    return jax.shard_map(
        on_device, mesh=mesh, in_specs=in_specs, out_specs=P("dp", "seq", None), check_vma=False
    )
```

```python
import functools
import math

import jax
import jax.numpy as jnp
from jax import lax
from jax.experimental import pallas as pl
from jax.experimental.pallas import tpu as pltpu
from jax.sharding import PartitionSpec as P

HEADS = 8
HEAD_DIM = 72
HD = HEADS * HEAD_DIM
SECTION = 640
NFD = 7
EPS = 1e-06
LOW = -1e30
NT = (((1,), (1,)), ((), ()))


def block_kernel(groups, x_ref, mod_ref, w_ref, wo_ref, rows_ref, cols_ref, o_ref, qkv_ref, s_ref, p_ref, mix_ref):
    values = x_ref[...].astype(jnp.float32)
    center = values - jnp.mean(values, axis=-1, keepdims=True)
    spread = jnp.mean(center * center, axis=-1, keepdims=True)
    normed = center * lax.rsqrt(spread + EPS) * (1.0 + mod_ref[1:2, :]) + mod_ref[0:1, :]
    normed = normed.astype(jnp.bfloat16)
    for part in range(3):
        start = part * SECTION
        qkv_ref[:, start + SECTION - 128 : start + SECTION] = jnp.zeros((values.shape[0], 128), jnp.bfloat16)
        qkv_ref[:, start : start + HD] = lax.dot_general(
            normed, w_ref[part * HD : (part + 1) * HD, :], NT, preferred_element_type=jnp.float32
        ).astype(jnp.bfloat16)
    mix_ref[...] = jnp.zeros_like(mix_ref)
    factor = 1.0 / math.sqrt(HEAD_DIM)
    lane = lax.broadcasted_iota(jnp.int32, (1, 256), 1)
    tasks = [(h, start, size) for start, size in groups for h in range(HEADS)]

    def window(h):
        base = (HEAD_DIM * h) // 128 * 128
        low = HEAD_DIM * h - base
        return base, (lane >= low) & (lane < low + HEAD_DIM)

    def scores(t):
        h, start, size = tasks[t]
        base, own = window(h)
        rows = pl.ds(start, size)
        q = jnp.where(own, qkv_ref[rows, pl.ds(base, 256)], jnp.bfloat16(0))
        k = qkv_ref[rows, pl.ds(SECTION + base, 256)]
        s_ref[t % 2, :size, :size] = lax.dot_general(q, k, NT, preferred_element_type=jnp.float32)

    def weights(t):
        h, start, size = tasks[t]
        same = rows_ref[start : start + size, 0:1] == cols_ref[0:1, start : start + size]
        s = jnp.where(same, s_ref[t % 2, :size, :size] * factor, LOW)
        raised = jnp.exp(s - jnp.max(s, axis=-1, keepdims=True))
        p_ref[t % 2, :size, :size] = (raised / jnp.sum(raised, axis=-1, keepdims=True)).astype(jnp.bfloat16)

    def mixing(t):
        h, start, size = tasks[t]
        base, own = window(h)
        rows = pl.ds(start, size)
        mixed = jnp.dot(
            p_ref[t % 2, :size, :size],
            qkv_ref[rows, pl.ds(2 * SECTION + base, 256)],
            preferred_element_type=jnp.float32,
        ).astype(jnp.bfloat16)
        mix_ref[rows, pl.ds(base, 256)] = jnp.where(own, mixed, mix_ref[rows, pl.ds(base, 256)])

    scores(0)
    for t in range(len(tasks)):
        if t + 1 < len(tasks):
            scores(t + 1)
        weights(t)
        mixing(t)
    projected = jnp.dot(mix_ref[:, 0:HD], wo_ref[...], preferred_element_type=jnp.float32)
    o_ref[...] = (x_ref[...].astype(jnp.float32) + mod_ref[2:3, :] * projected).astype(jnp.bfloat16)


def block(x, mod, w_qkv, w_out, ids, groups):
    rows, width = x.shape
    biggest = max(size for _, size in groups)
    vmem = pl.BlockSpec(memory_space=pltpu.VMEM)
    return pl.pallas_call(
        functools.partial(block_kernel, groups),
        out_shape=jax.ShapeDtypeStruct(x.shape, x.dtype),
        in_specs=[vmem] * 6,
        out_specs=vmem,
        scratch_shapes=[
            pltpu.VMEM((rows, 3 * SECTION), jnp.bfloat16),
            pltpu.VMEM((2, biggest, biggest), jnp.float32),
            pltpu.VMEM((2, biggest, biggest), jnp.bfloat16),
            pltpu.VMEM((rows, SECTION), jnp.bfloat16),
        ],
        compiler_params=pltpu.CompilerParams(vmem_limit_bytes=26 * 1024 * 1024),
        cost_estimate=pl.CostEstimate(
            flops=2 * rows * width * (3 * SECTION + SECTION) + 4 * HEADS * rows * biggest * 256,
            bytes_accessed=2 * 2 * rows * width + 2 * 4 * SECTION * width,
            transcendentals=HEADS * rows * biggest,
        ),
    )(x, mod, w_qkv, w_out, ids.reshape(-1, 1), ids.reshape(1, -1))


def source_index(counts, dest):
    groups, slots = dest.shape
    slot_ids = jnp.arange(slots, dtype=jnp.int32)
    live = slot_ids[None, :] < counts[:, None]
    targets = jnp.where(live, dest, -1).reshape(-1)
    wanted = jnp.arange(groups * NFD, dtype=jnp.int32)
    anchors = jnp.arange(groups * slots, dtype=jnp.int32)
    return jnp.sum(jnp.where(targets[None, :] == wanted[:, None], anchors[None, :], 0), axis=1)


def on_device(slot_tokens, modulation, counts, dest, qkv_spatial, out_spatial, qkv_temporal, out_temporal):
    groups = lax.axis_size("dp")
    shards = lax.axis_size("seq")
    slots, patches, width = slot_tokens.shape
    piece = patches // groups
    mod = modulation[0]
    pieces = slot_tokens.reshape(slots, groups, piece, width).transpose(1, 0, 2, 3)
    spread = lax.all_to_all(pieces, "dp", split_axis=0, concat_axis=0, tiled=True)
    chosen = jnp.take(
        spread.reshape(groups * slots, piece, width), source_index(counts, dest), axis=0, mode="clip"
    )
    gathered = lax.all_to_all(
        chosen.reshape(groups, NFD, piece, width), "dp", split_axis=0, concat_axis=0, tiled=True
    )
    frames = gathered.transpose(1, 0, 2, 3).reshape(NFD * patches, width)
    row = jnp.arange(NFD * patches, dtype=jnp.int32)
    after = block(
        frames,
        mod[0:3],
        qkv_spatial.T,
        out_spatial,
        row // patches,
        ((0, 4 * patches), (4 * patches, 3 * patches)),
    )
    widest = patches // shards
    total = shards * NFD
    moved = lax.all_to_all(
        after.reshape(NFD, shards, widest, width), "seq", split_axis=1, concat_axis=0, tiled=True
    )
    home = block(
        moved.reshape(total * widest, width),
        mod[3:6],
        qkv_temporal.T,
        out_temporal,
        row % widest,
        ((0, total * widest),),
    )
    back = lax.all_to_all(
        home.reshape(total, 1, widest, width), "seq", split_axis=0, concat_axis=1, tiled=True
    )
    return back.reshape(NFD, patches, width)


def solution(mesh):
    in_specs = (P("dp", "seq", None), P("dp", None, None), P(), P(), P(), P(), P(), P())
    return jax.shard_map(
        on_device, mesh=mesh, in_specs=in_specs, out_specs=P("dp", "seq", None), check_vma=False
    )
```

```python
import functools
import math

import jax
import jax.numpy as jnp
from jax import lax
from jax.experimental import pallas as pl
from jax.experimental.pallas import tpu as pltpu
from jax.sharding import PartitionSpec as P

HEADS = 8
HEAD_DIM = 72
HD = HEADS * HEAD_DIM
SECTION = 640
NFD = 7
EPS = 1e-06
LOW = -1e30
NT = (((1,), (1,)), ((), ()))
VMEM = pl.BlockSpec(memory_space=pltpu.VMEM)
HBM = pl.BlockSpec(memory_space=pltpu.HBM)
SMEM = pl.BlockSpec(memory_space=pltpu.SMEM)


def limit(mib):
    return pltpu.CompilerParams(vmem_limit_bytes=mib * 1024 * 1024)


def spread_kernel(x_ref, o_ref):
    slots = x_ref.shape[0]
    for q in range(slots):
        o_ref[:, q] = x_ref[q].reshape(o_ref.shape[0], 2, x_ref.shape[2])


def spread_pieces(slot_tokens, groups):
    slots, patches, width = slot_tokens.shape
    steps = 4
    return pl.pallas_call(
        spread_kernel,
        out_shape=jax.ShapeDtypeStruct((groups, slots, 2, width), slot_tokens.dtype),
        grid=(steps,),
        in_specs=[pl.BlockSpec((slots, patches // steps, width), lambda i: (0, i, 0))],
        out_specs=pl.BlockSpec((groups // steps, slots, 2, width), lambda i: (i, 0, 0, 0)),
        compiler_params=limit(63),
    )(slot_tokens)


def choose_kernel(index_ref, x_ref, o_ref):
    unroll = 8

    def body(i, carry):
        for j in range(unroll):
            o_ref[i * unroll + j] = x_ref[index_ref[i * unroll + j]]
        return carry

    lax.fori_loop(0, o_ref.shape[0] // unroll, body, 0)


def choose_pieces(spread, index):
    return pl.pallas_call(
        choose_kernel,
        out_shape=jax.ShapeDtypeStruct((index.shape[0],) + spread.shape[1:], spread.dtype),
        in_specs=[SMEM, VMEM],
        out_specs=VMEM,
        compiler_params=limit(26),
    )(index, spread)


def normalized(values, mod_ref):
    center = values - jnp.mean(values, axis=-1, keepdims=True)
    spread = jnp.mean(center * center, axis=-1, keepdims=True)
    return center * lax.rsqrt(spread + EPS) * (1.0 + mod_ref[1:2, :]) + mod_ref[0:1, :]


def project_qkv(normed, w_ref, waits, qkv_ref):
    for part in range(3):
        start = part * SECTION
        qkv_ref[:, start + SECTION - 128 : start + SECTION] = jnp.zeros((normed.shape[0], 128), jnp.bfloat16)
        waits[part].wait()
        qkv_ref[:, start : start + HD] = lax.dot_general(
            normed, w_ref[part * HD : (part + 1) * HD, :], NT, preferred_element_type=jnp.float32
        ).astype(jnp.bfloat16)


def attend(groups, rows_ref, cols_ref, qkv_ref, s_ref, p_ref, mix_ref):
    factor = 1.0 / math.sqrt(HEAD_DIM)
    lane = lax.broadcasted_iota(jnp.int32, (1, 256), 1)
    tasks = [(h, start, size) for start, size in groups for h in range(HEADS)]

    def window(h):
        base = (HEAD_DIM * h) // 128 * 128
        low = HEAD_DIM * h - base
        return base, (lane >= low) & (lane < low + HEAD_DIM)

    def scores(t):
        h, start, size = tasks[t]
        base, own = window(h)
        rows = pl.ds(start, size)
        q = jnp.where(own, qkv_ref[rows, pl.ds(base, 256)], jnp.bfloat16(0))
        k = qkv_ref[rows, pl.ds(SECTION + base, 256)]
        s_ref[t % 2, :size, :size] = lax.dot_general(q, k, NT, preferred_element_type=jnp.float32)

    def weights(t):
        h, start, size = tasks[t]
        same = rows_ref[start : start + size, 0:1] == cols_ref[0:1, start : start + size]
        s = jnp.where(same, s_ref[t % 2, :size, :size] * factor, LOW)
        raised = jnp.exp(s - jnp.max(s, axis=-1, keepdims=True))
        p_ref[t % 2, :size, :size] = (raised / jnp.sum(raised, axis=-1, keepdims=True)).astype(jnp.bfloat16)

    def mixing(t):
        h, start, size = tasks[t]
        base, own = window(h)
        rows = pl.ds(start, size)
        mixed = jnp.dot(
            p_ref[t % 2, :size, :size],
            qkv_ref[rows, pl.ds(2 * SECTION + base, 256)],
            preferred_element_type=jnp.float32,
        ).astype(jnp.bfloat16)
        mix_ref[rows, pl.ds(base, 256)] = jnp.where(own, mixed, mix_ref[rows, pl.ds(base, 256)])

    scores(0)
    for t in range(len(tasks)):
        if t + 1 < len(tasks):
            scores(t + 1)
        weights(t)
        mixing(t)


def fetch_qkv(w_hbm, w_ref, sems):
    copies = [
        pltpu.make_async_copy(
            w_hbm.at[pl.ds(part * HD, HD)], w_ref.at[pl.ds(part * HD, HD)], sems.at[part]
        )
        for part in range(3)
    ]
    for copy in copies:
        copy.start()
    return copies


def spatial_kernel(
    groups, x_ref, mod_ref, w_hbm, wo_hbm, rows_ref, cols_ref, o_ref,
    frames_ref, w_ref, wo_ref, qkv_ref, s_ref, p_ref, mix_ref, sems,
):
    copies = fetch_qkv(w_hbm, w_ref, sems)
    last = pltpu.make_async_copy(wo_hbm, wo_ref, sems.at[3])
    last.start()
    frame_count = x_ref.shape[1]
    patches = frames_ref.shape[0] // frame_count
    for k in range(frame_count):
        frames_ref[k * patches : (k + 1) * patches] = x_ref[:, k].reshape(patches, x_ref.shape[3])
    values = frames_ref[...].astype(jnp.float32)
    project_qkv(normalized(values, mod_ref).astype(jnp.bfloat16), w_ref, copies, qkv_ref)
    mix_ref[...] = jnp.zeros_like(mix_ref)
    attend(groups, rows_ref, cols_ref, qkv_ref, s_ref, p_ref, mix_ref)
    last.wait()
    shards = o_ref.shape[0]
    widest = patches // shards
    for k in range(frame_count):
        rows = pl.ds(k * patches, patches)
        projected = jnp.dot(mix_ref[rows, 0:HD], wo_ref[...], preferred_element_type=jnp.float32)
        after = frames_ref[rows, :].astype(jnp.float32) + mod_ref[2:3, :] * projected
        for j in range(shards):
            o_ref[j, k * widest : (k + 1) * widest, :] = after[j * widest : (j + 1) * widest].astype(jnp.bfloat16)


def spatial_block(gathered, mod, w_qkv, w_out, ids, groups, shards):
    pieces, frame_count, piece, width = gathered.shape
    rows = pieces * frame_count * piece
    biggest = max(size for _, size in groups)
    return pl.pallas_call(
        functools.partial(spatial_kernel, groups),
        out_shape=jax.ShapeDtypeStruct((shards, rows // shards, width), gathered.dtype),
        in_specs=[VMEM, VMEM, HBM, HBM, VMEM, VMEM],
        out_specs=VMEM,
        scratch_shapes=[
            pltpu.VMEM((rows, width), jnp.bfloat16),
            pltpu.VMEM(w_qkv.shape, jnp.bfloat16),
            pltpu.VMEM(w_out.shape, jnp.bfloat16),
            pltpu.VMEM((rows, 3 * SECTION), jnp.bfloat16),
            pltpu.VMEM((2, biggest, biggest), jnp.float32),
            pltpu.VMEM((2, biggest, biggest), jnp.bfloat16),
            pltpu.VMEM((rows, SECTION), jnp.bfloat16),
            pltpu.SemaphoreType.DMA((4,)),
        ],
        compiler_params=limit(51),
    )(gathered, mod, w_qkv, w_out, ids.reshape(-1, 1), ids.reshape(1, -1))


def temporal_kernel(
    groups, x_ref, mod_ref, w_hbm, rows_ref, cols_ref, o_ref, w_ref, qkv_ref, s_ref, p_ref, mix_ref, sems
):
    copies = fetch_qkv(w_hbm, w_ref, sems)
    values = x_ref[...].astype(jnp.float32)
    project_qkv(normalized(values, mod_ref).astype(jnp.bfloat16), w_ref, copies, qkv_ref)
    mix_ref[...] = jnp.zeros_like(mix_ref)
    attend(groups, rows_ref, cols_ref, qkv_ref, s_ref, p_ref, mix_ref)
    o_ref[...] = mix_ref[:, 0:HD]


def temporal_block(x, mod, w_qkv, ids, groups):
    rows, width = x.shape
    biggest = max(size for _, size in groups)
    return pl.pallas_call(
        functools.partial(temporal_kernel, groups),
        out_shape=jax.ShapeDtypeStruct((rows, HD), x.dtype),
        in_specs=[VMEM, VMEM, HBM, VMEM, VMEM],
        out_specs=VMEM,
        scratch_shapes=[
            pltpu.VMEM(w_qkv.shape, jnp.bfloat16),
            pltpu.VMEM((rows, 3 * SECTION), jnp.bfloat16),
            pltpu.VMEM((2, biggest, biggest), jnp.float32),
            pltpu.VMEM((2, biggest, biggest), jnp.bfloat16),
            pltpu.VMEM((rows, SECTION), jnp.bfloat16),
            pltpu.SemaphoreType.DMA((3,)),
        ],
        compiler_params=limit(52),
    )(x, mod, w_qkv, ids.reshape(-1, 1), ids.reshape(1, -1))


def final_kernel(mixed_ref, after_ref, mod_ref, wo_ref, o_ref):
    frame_count, patches, _ = o_ref.shape
    shards = after_ref.shape[0]
    widest = patches // shards
    for j in range(shards):
        projected = jnp.dot(mixed_ref[j], wo_ref[...], preferred_element_type=jnp.float32)
        result = after_ref[j].astype(jnp.float32) + mod_ref[2:3, :] * projected
        for k in range(frame_count):
            o_ref[k, j * widest : (j + 1) * widest, :] = result[k * widest : (k + 1) * widest].astype(jnp.bfloat16)


def final_block(mixed, after, mod, w_out):
    shards, rows, width = after.shape
    return pl.pallas_call(
        final_kernel,
        out_shape=jax.ShapeDtypeStruct((NFD, shards * rows // NFD, width), after.dtype),
        in_specs=[VMEM] * 4,
        out_specs=VMEM,
        compiler_params=limit(26),
    )(mixed, after, mod, w_out)


def source_index(counts, dest):
    groups, slots = dest.shape
    slot_ids = jnp.arange(slots, dtype=jnp.int32)
    live = slot_ids[None, :] < counts[:, None]
    targets = jnp.where(live, dest, -1).reshape(-1)
    wanted = jnp.arange(groups * NFD, dtype=jnp.int32)
    anchors = jnp.arange(groups * slots, dtype=jnp.int32)
    return jnp.sum(jnp.where(targets[None, :] == wanted[:, None], anchors[None, :], 0), axis=1)


def on_device(slot_tokens, modulation, counts, dest, qkv_spatial, out_spatial, qkv_temporal, out_temporal):
    groups = lax.axis_size("dp")
    shards = lax.axis_size("seq")
    slots, patches, width = slot_tokens.shape
    piece = patches // groups
    mod = modulation[0]
    spread = lax.all_to_all(spread_pieces(slot_tokens, groups), "dp", split_axis=0, concat_axis=0, tiled=True)
    chosen = choose_pieces(spread.reshape(groups * slots, piece, width), source_index(counts, dest))
    gathered = lax.all_to_all(
        chosen.reshape(groups, NFD, piece, width), "dp", split_axis=0, concat_axis=0, tiled=True
    )
    row = jnp.arange(NFD * patches, dtype=jnp.int32)
    after = spatial_block(
        gathered,
        mod[0:3],
        qkv_spatial.T,
        out_spatial,
        row // patches,
        ((0, 4 * patches), (4 * patches, 3 * patches)),
        shards,
    )
    widest = patches // shards
    moved = lax.all_to_all(after, "seq", split_axis=0, concat_axis=0, tiled=True)
    mixed = temporal_block(
        moved.reshape(NFD * patches, width), mod[3:6], qkv_temporal.T, row % widest, ((0, NFD * patches),)
    )
    back = lax.all_to_all(
        mixed.reshape(shards, NFD * widest, HD), "seq", split_axis=0, concat_axis=0, tiled=True
    )
    return final_block(back, after, mod[3:6], out_temporal)


def solution(mesh):
    in_specs = (P("dp", "seq", None), P("dp", None, None), P(), P(), P(), P(), P(), P())
    return jax.shard_map(
        on_device, mesh=mesh, in_specs=in_specs, out_specs=P("dp", "seq", None), check_vma=False
    )
```

```python
import functools
import math

import jax
import jax.numpy as jnp
from jax import lax
from jax.experimental import pallas as pl
from jax.experimental.pallas import tpu as pltpu
from jax.sharding import PartitionSpec as P

HEADS = 8
HEAD_DIM = 72
HD = HEADS * HEAD_DIM
SECTION = 640
NFD = 7
EPS = 1e-06
LOW = -1e30
NT = (((1,), (1,)), ((), ()))
VMEM = pl.BlockSpec(memory_space=pltpu.VMEM)
SMEM = pl.BlockSpec(memory_space=pltpu.SMEM)


def limit(mib):
    return pltpu.CompilerParams(vmem_limit_bytes=mib * 1024 * 1024)


def spread_kernel(x_ref, o_ref):
    slots = x_ref.shape[0]
    for q in range(slots):
        o_ref[:, q] = x_ref[q].reshape(o_ref.shape[0], 2, x_ref.shape[2])


def spread_pieces(slot_tokens, groups):
    slots, patches, width = slot_tokens.shape
    steps = 4
    return pl.pallas_call(
        spread_kernel,
        out_shape=jax.ShapeDtypeStruct((groups, slots, 2, width), slot_tokens.dtype),
        grid=(steps,),
        in_specs=[pl.BlockSpec((slots, patches // steps, width), lambda i: (0, i, 0))],
        out_specs=pl.BlockSpec((groups // steps, slots, 2, width), lambda i: (i, 0, 0, 0)),
        compiler_params=limit(63),
    )(slot_tokens)


def choose_kernel(index_ref, x_ref, o_ref):
    unroll = 8

    def body(i, carry):
        for j in range(unroll):
            o_ref[i * unroll + j] = x_ref[index_ref[i * unroll + j]]
        return carry

    lax.fori_loop(0, o_ref.shape[0] // unroll, body, 0)


def choose_pieces(spread, index):
    return pl.pallas_call(
        choose_kernel,
        out_shape=jax.ShapeDtypeStruct((index.shape[0],) + spread.shape[1:], spread.dtype),
        in_specs=[SMEM, VMEM],
        out_specs=VMEM,
        compiler_params=limit(26),
    )(index, spread)


def normalize(load, mod_ref, base, normed_ref):
    step = 16
    scale = 1.0 + mod_ref[base + 1 : base + 2, :]
    shift = mod_ref[base : base + 1, :]
    for at in range(0, normed_ref.shape[0], step):
        values = load(at, step).astype(jnp.float32)
        center = values - jnp.mean(values, axis=-1, keepdims=True)
        spread = jnp.mean(center * center, axis=-1, keepdims=True)
        normed_ref[at : at + step] = (center * lax.rsqrt(spread + EPS) * scale + shift).astype(jnp.bfloat16)


def project_qkv(normed_ref, w_ref, qkv_ref):
    normed = normed_ref[...]
    for part in range(3):
        start = part * SECTION
        qkv_ref[:, start + SECTION - 128 : start + SECTION] = jnp.zeros((normed.shape[0], 128), jnp.bfloat16)
    rows = normed.shape[0] // 2
    for at in range(0, 2 * rows, rows):
        full = lax.dot_general(normed[at : at + rows], w_ref[...], NT, preferred_element_type=jnp.float32)
        for part in range(3):
            qkv_ref[at : at + rows, part * SECTION : part * SECTION + HD] = full[
                :, part * HD : (part + 1) * HD
            ].astype(jnp.bfloat16)


def attend(groups, group_of, qkv_ref, s_ref, p_ref, mix_ref):
    factor = math.log2(math.e) / math.sqrt(HEAD_DIM)
    lane = lax.broadcasted_iota(jnp.int32, (1, 256), 1)
    tasks = [(h, start, size) for start, size in groups for h in range(HEADS)]

    def window(h):
        base = (HEAD_DIM * h) // 128 * 128
        low = HEAD_DIM * h - base
        return base, (lane >= low) & (lane < low + HEAD_DIM)

    def scores(t):
        h, start, size = tasks[t]
        base, own = window(h)
        rows = pl.ds(start, size)
        q = jnp.where(own, qkv_ref[rows, pl.ds(base, 256)], jnp.bfloat16(0))
        k = qkv_ref[rows, pl.ds(SECTION + base, 256)]
        s_ref[t % 2, :size, :size] = lax.dot_general(q, k, NT, preferred_element_type=jnp.float32)

    def weights(t):
        h, start, size = tasks[t]
        same = group_of(lax.broadcasted_iota(jnp.int32, (size, 1), 0)) == group_of(
            lax.broadcasted_iota(jnp.int32, (1, size), 1)
        )
        s = jnp.where(same, s_ref[t % 2, :size, :size], LOW)
        raised = jnp.exp2((s - jnp.max(s, axis=-1, keepdims=True)) * factor)
        inverse = 1.0 / jnp.sum(raised, axis=-1, keepdims=True)
        p_ref[t % 2, :size, :size] = (raised * inverse).astype(jnp.bfloat16)

    def mixing(t):
        h, start, size = tasks[t]
        base, own = window(h)
        rows = pl.ds(start, size)
        mixed = jnp.dot(
            p_ref[t % 2, :size, :size],
            qkv_ref[rows, pl.ds(2 * SECTION + base, 256)],
            preferred_element_type=jnp.float32,
        ).astype(jnp.bfloat16)
        mix_ref[rows, pl.ds(base, 256)] = jnp.where(own, mixed, mix_ref[rows, pl.ds(base, 256)])

    scores(0)
    for t in range(len(tasks)):
        if t + 1 < len(tasks):
            scores(t + 1)
        weights(t)
        mixing(t)


def spatial_kernel(
    groups, group_of, x_ref, mod_ref, w_ref, wo_ref, o_ref, frames_ref, normed_ref, qkv_ref, s_ref, p_ref, mix_ref
):
    frame_count = x_ref.shape[1]
    patches = frames_ref.shape[0] // frame_count

    def load(at, step):
        k, w = at // patches, at % patches // 2
        rows = x_ref[w : w + step // 2, k].reshape(step, x_ref.shape[3])
        frames_ref[at : at + step] = rows
        return rows

    normalize(load, mod_ref, 0, normed_ref)
    project_qkv(normed_ref, w_ref, qkv_ref)
    mix_ref[...] = jnp.zeros_like(mix_ref)
    attend(groups, group_of, qkv_ref, s_ref, p_ref, mix_ref)
    shards = o_ref.shape[0]
    widest = patches // shards
    for start, size in groups:
        rows = pl.ds(start, size)
        projected = jnp.dot(mix_ref[rows, 0:HD], wo_ref[...], preferred_element_type=jnp.float32)
        after = (frames_ref[rows, :].astype(jnp.float32) + mod_ref[2:3, :] * projected).astype(jnp.bfloat16)
        for at in range(0, size, widest):
            k, j = (start + at) // patches, (start + at) % patches // widest
            o_ref[j, k * widest : (k + 1) * widest, :] = after[at : at + widest]


def spatial_block(gathered, mod, w_qkv, w_out, groups, group_of, shards):
    pieces, frame_count, piece, width = gathered.shape
    rows = pieces * frame_count * piece
    biggest = max(size for _, size in groups)
    return pl.pallas_call(
        functools.partial(spatial_kernel, groups, group_of),
        out_shape=jax.ShapeDtypeStruct((shards, rows // shards, width), gathered.dtype),
        in_specs=[VMEM] * 4,
        out_specs=VMEM,
        scratch_shapes=[
            pltpu.VMEM((rows, width), jnp.bfloat16),
            pltpu.VMEM((rows, width), jnp.bfloat16),
            pltpu.VMEM((rows, 3 * SECTION), jnp.bfloat16),
            pltpu.VMEM((2, biggest, biggest), jnp.float32),
            pltpu.VMEM((2, biggest, biggest), jnp.bfloat16),
            pltpu.VMEM((rows, SECTION), jnp.bfloat16),
        ],
        compiler_params=limit(28),
    )(gathered, mod, w_qkv, w_out)


def temporal_kernel(
    groups, group_of, x_ref, mod_ref, w_ref, o_ref, normed_ref, qkv_ref, s_ref, p_ref, mix_ref
):
    normalize(lambda at, step: x_ref[at : at + step], mod_ref, 3, normed_ref)
    project_qkv(normed_ref, w_ref, qkv_ref)
    mix_ref[...] = jnp.zeros_like(mix_ref)
    attend(groups, group_of, qkv_ref, s_ref, p_ref, mix_ref)
    o_ref[...] = mix_ref[:, 0:HD]


def temporal_block(x, mod, w_qkv, groups, group_of):
    rows, width = x.shape
    biggest = max(size for _, size in groups)
    return pl.pallas_call(
        functools.partial(temporal_kernel, groups, group_of),
        out_shape=jax.ShapeDtypeStruct((rows, HD), x.dtype),
        in_specs=[VMEM] * 3,
        out_specs=VMEM,
        scratch_shapes=[
            pltpu.VMEM((rows, width), jnp.bfloat16),
            pltpu.VMEM((rows, 3 * SECTION), jnp.bfloat16),
            pltpu.VMEM((2, biggest, biggest), jnp.float32),
            pltpu.VMEM((2, biggest, biggest), jnp.bfloat16),
            pltpu.VMEM((rows, SECTION), jnp.bfloat16),
        ],
        compiler_params=limit(28),
    )(x, mod, w_qkv)


def final_kernel(mixed_ref, after_ref, mod_ref, wo_ref, o_ref):
    frame_count, patches, _ = o_ref.shape
    shards = after_ref.shape[0]
    widest = patches // shards
    rows = after_ref.shape[1]
    half = shards // 2
    for first in range(0, shards, half):
        mixed = mixed_ref[first : first + half].reshape(half * rows, mixed_ref.shape[2])
        projected = jnp.dot(mixed, wo_ref[...], preferred_element_type=jnp.float32)
        for j in range(first, first + half):
            part = projected[(j - first) * rows : (j - first + 1) * rows]
            result = (after_ref[j].astype(jnp.float32) + mod_ref[5:6, :] * part).astype(jnp.bfloat16)
            for k in range(frame_count):
                o_ref[k, j * widest : (j + 1) * widest, :] = result[k * widest : (k + 1) * widest]


def final_block(mixed, after, mod, w_out):
    shards, rows, width = after.shape
    return pl.pallas_call(
        final_kernel,
        out_shape=jax.ShapeDtypeStruct((NFD, shards * rows // NFD, width), after.dtype),
        in_specs=[VMEM] * 4,
        out_specs=VMEM,
        compiler_params=limit(26),
    )(mixed, after, mod, w_out)


def source_index(counts, dest):
    groups, slots = dest.shape
    slot_ids = jnp.arange(slots, dtype=jnp.int32)
    live = slot_ids[None, :] < counts[:, None]
    targets = jnp.where(live, dest, -1).reshape(-1)
    wanted = jnp.arange(groups * NFD, dtype=jnp.int32)
    anchors = jnp.arange(groups * slots, dtype=jnp.int32)
    return jnp.sum(jnp.where(targets[None, :] == wanted[:, None], anchors[None, :], 0), axis=1)


def on_device(slot_tokens, modulation, counts, dest, qkv_spatial, out_spatial, qkv_temporal, out_temporal):
    groups = lax.axis_size("dp")
    shards = lax.axis_size("seq")
    slots, patches, width = slot_tokens.shape
    piece = patches // groups
    spread = lax.all_to_all(spread_pieces(slot_tokens, groups), "dp", split_axis=0, concat_axis=0, tiled=True)
    spread, mod, index = lax.optimization_barrier((spread, modulation[0], source_index(counts, dest)))
    chosen = choose_pieces(spread.reshape(groups * slots, piece, width), index)
    gathered = lax.all_to_all(
        chosen.reshape(groups, NFD, piece, width), "dp", split_axis=0, concat_axis=0, tiled=True
    )
    shift = patches.bit_length() - 1
    after = spatial_block(
        gathered,
        mod,
        qkv_spatial.T,
        out_spatial,
        ((0, 4 * patches), (4 * patches, 3 * patches)),
        lambda row: row >> shift,
        shards,
    )
    widest = patches // shards
    moved = lax.all_to_all(after, "seq", split_axis=0, concat_axis=0, tiled=True)
    mixed = temporal_block(
        moved.reshape(NFD * patches, width),
        mod,
        qkv_temporal.T,
        ((0, NFD * patches),),
        lambda row: row & (widest - 1),
    )
    back = lax.all_to_all(
        mixed.reshape(shards, NFD * widest, HD), "seq", split_axis=0, concat_axis=0, tiled=True
    )
    return final_block(back, after, mod, out_temporal)


def solution(mesh):
    in_specs = (P("dp", "seq", None), P("dp", None, None), P(), P(), P(), P(), P(), P())
    return jax.shard_map(
        on_device, mesh=mesh, in_specs=in_specs, out_specs=P("dp", "seq", None), check_vma=False
    )
```

```python
import functools
import math

import jax
import jax.numpy as jnp
from jax import lax
from jax.experimental import pallas as pl
from jax.experimental.pallas import tpu as pltpu
from jax.sharding import PartitionSpec as P

HEADS = 8
HEAD_DIM = 72
HD = HEADS * HEAD_DIM
SECTION = 640
NFD = 7
EPS = 1e-06
LOW = -1e30
CHIPS = 4
NT = (((1,), (1,)), ((), ()))
VMEM = pl.BlockSpec(memory_space=pltpu.VMEM)
ANY = pl.BlockSpec(memory_space=pl.ANY)
SMEM = pl.BlockSpec(memory_space=pltpu.SMEM)


def limit(mib):
    return pltpu.CompilerParams(vmem_limit_bytes=mib * 1024 * 1024)


def spread_kernel(x_hbm, o_hbm, x_ref, o_ref, in_sems, out_sems):
    slots, patches, width = x_ref.shape
    groups = o_ref.shape[1]
    loads = [pltpu.make_async_copy(x_hbm.at[q], x_ref.at[q], in_sems.at[q]) for q in range(slots)]
    stores = [pltpu.make_async_copy(o_ref.at[q], o_hbm.at[:, q], out_sems.at[q]) for q in range(slots)]
    for load in loads:
        load.start()
    for q in range(slots):
        loads[q].wait()
        o_ref[q] = x_ref[q].reshape(groups, patches // groups, width)
        stores[q].start()
    for store in stores:
        store.wait()


def spread_pieces(slot_tokens, groups):
    slots, patches, width = slot_tokens.shape
    piece = patches // groups
    dtype = slot_tokens.dtype
    return pl.pallas_call(
        spread_kernel,
        out_shape=jax.ShapeDtypeStruct((groups, slots, piece, width), dtype),
        in_specs=[ANY],
        out_specs=ANY,
        scratch_shapes=[
            pltpu.VMEM((slots, patches, width), dtype),
            pltpu.VMEM((slots, groups, piece, width), dtype),
            pltpu.SemaphoreType.DMA((slots,)),
            pltpu.SemaphoreType.DMA((slots,)),
        ],
        compiler_params=limit(63),
    )(slot_tokens)


def choose_kernel(index_ref, x_ref, o_ref):
    unroll = 8

    def body(i, carry):
        for j in range(unroll):
            o_ref[i * unroll + j] = x_ref[index_ref[i * unroll + j]]
        return carry

    lax.fori_loop(0, o_ref.shape[0] // unroll, body, 0)


def choose_pieces(spread, index):
    return pl.pallas_call(
        choose_kernel,
        out_shape=jax.ShapeDtypeStruct((index.shape[0],) + spread.shape[1:], spread.dtype),
        in_specs=[SMEM, VMEM],
        out_specs=VMEM,
        compiler_params=limit(26),
    )(index, spread)


def normalize(load, mod_ref, base, normed_ref):
    total = normed_ref.shape[0]
    scale = 1.0 + mod_ref[base + 1 : base + 2, :]
    shift = mod_ref[base : base + 1, :]
    for at in range(0, total, 16):
        step = min(16, total - at)
        values = load(at, step).astype(jnp.float32)
        center = values - jnp.mean(values, axis=-1, keepdims=True)
        spread = jnp.mean(center * center, axis=-1, keepdims=True)
        normed_ref[at : at + step] = (center * lax.rsqrt(spread + EPS) * scale + shift).astype(jnp.bfloat16)


def project_qkv(normed_ref, w_ref, qkv_ref):
    normed = normed_ref[...]
    for part in range(3):
        start = part * SECTION
        qkv_ref[:, start + SECTION - 128 : start + SECTION] = jnp.zeros((normed.shape[0], 128), jnp.bfloat16)
    rows = normed.shape[0] // 2
    for at in range(0, 2 * rows, rows):
        full = lax.dot_general(normed[at : at + rows], w_ref[...], NT, preferred_element_type=jnp.float32)
        for part in range(3):
            qkv_ref[at : at + rows, part * SECTION : part * SECTION + HD] = full[
                :, part * HD : (part + 1) * HD
            ].astype(jnp.bfloat16)


def attend(groups, group_of, qkv_ref, s_ref, p_ref, mix_ref):
    factor = math.log2(math.e) / math.sqrt(HEAD_DIM)
    lane = lax.broadcasted_iota(jnp.int32, (1, 256), 1)
    tasks = [(h, start, size) for start, size in groups for h in range(HEADS)]

    def window(h):
        base = (HEAD_DIM * h) // 128 * 128
        low = HEAD_DIM * h - base
        return base, (lane >= low) & (lane < low + HEAD_DIM)

    def scores(t):
        h, start, size = tasks[t]
        base, own = window(h)
        rows = pl.ds(start, size)
        q = jnp.where(own, qkv_ref[rows, pl.ds(base, 256)], jnp.bfloat16(0))
        k = qkv_ref[rows, pl.ds(SECTION + base, 256)]
        s_ref[t % 2, :size, :size] = lax.dot_general(q, k, NT, preferred_element_type=jnp.float32)

    def weights(t):
        h, start, size = tasks[t]
        same = group_of(lax.broadcasted_iota(jnp.int32, (size, 1), 0)) == group_of(
            lax.broadcasted_iota(jnp.int32, (1, size), 1)
        )
        s = jnp.where(same, s_ref[t % 2, :size, :size], LOW)
        raised = jnp.exp2((s - jnp.max(s, axis=-1, keepdims=True)) * factor)
        inverse = 1.0 / jnp.sum(raised, axis=-1, keepdims=True)
        p_ref[t % 2, :size, :size] = (raised * inverse).astype(jnp.bfloat16)

    def mixing(t):
        h, start, size = tasks[t]
        base, own = window(h)
        rows = pl.ds(start, size)
        mixed = jnp.dot(
            p_ref[t % 2, :size, :size],
            qkv_ref[rows, pl.ds(2 * SECTION + base, 256)],
            preferred_element_type=jnp.float32,
        ).astype(jnp.bfloat16)
        mix_ref[rows, pl.ds(base, 256)] = jnp.where(own, mixed, mix_ref[rows, pl.ds(base, 256)])

    scores(0)
    for t in range(len(tasks)):
        if t + 1 < len(tasks):
            scores(t + 1)
        weights(t)
        mixing(t)


def sent(refs):
    far = refs[2:]
    return [refs[0]] + [ref.at[0] for ref in far] + [refs[1]] + [ref.at[1] for ref in far]


def sent_shapes(rows, width, dtype):
    near, far = jax.ShapeDtypeStruct((rows, width), dtype), jax.ShapeDtypeStruct((2, rows, width), dtype)
    return [near] * 2 + [far] * (CHIPS - 1)


def arrived(refs):
    return [refs[0]] + [ref.at[0] for ref in refs[1:CHIPS]] + list(refs[CHIPS:])


def spatial_kernel(
    groups, group_of, place_ref, x_ref, mod_ref, w_ref, wo_ref, *refs
):
    o_refs, (frames_ref, normed_ref, qkv_ref, s_ref, p_ref, mix_ref, after_ref) = refs[: CHIPS + 1], refs[CHIPS + 1 :]
    outgoing = sent(o_refs)
    frame_count = x_ref.shape[1]
    patches = frames_ref.shape[0] // frame_count

    def load(at, step):
        k, w = at // patches, at % patches // 2
        rows = x_ref[w : w + step // 2, k].reshape(step, x_ref.shape[3])
        frames_ref[at : at + step] = rows
        return rows

    normalize(load, mod_ref, 0, normed_ref)
    project_qkv(normed_ref, w_ref, qkv_ref)
    mix_ref[...] = jnp.zeros_like(mix_ref)
    attend(groups, group_of, qkv_ref, s_ref, p_ref, mix_ref)
    shards = after_ref.shape[0]
    widest = patches // shards
    for start, size in groups:
        rows = pl.ds(start, size)
        projected = jnp.dot(mix_ref[rows, 0:HD], wo_ref[...], preferred_element_type=jnp.float32)
        after = (frames_ref[rows, :].astype(jnp.float32) + mod_ref[2:3, :] * projected).astype(jnp.bfloat16)
        for at in range(0, size, widest):
            k, j = (start + at) // patches, (start + at) % patches // widest
            after_ref[j, k * widest : (k + 1) * widest, :] = after[at : at + widest]
    for d in range(CHIPS):
        chip = 2 * ((place_ref[0] + d) & (CHIPS - 1))
        outgoing[d][...] = after_ref[chip + place_ref[1]]
        outgoing[CHIPS + d][...] = after_ref[chip + 1 - place_ref[1]]


def spatial_block(place, gathered, mod, w_qkv, w_out, groups, group_of, shards):
    pieces, frame_count, piece, width = gathered.shape
    rows = pieces * frame_count * piece
    biggest = max(size for _, size in groups)
    return pl.pallas_call(
        functools.partial(spatial_kernel, groups, group_of),
        out_shape=sent_shapes(rows // shards, width, gathered.dtype),
        in_specs=[SMEM] + [VMEM] * 4,
        out_specs=[VMEM] * (CHIPS + 1),
        scratch_shapes=[
            pltpu.VMEM((rows, width), jnp.bfloat16),
            pltpu.VMEM((rows, width), jnp.bfloat16),
            pltpu.VMEM((rows, 3 * SECTION), jnp.bfloat16),
            pltpu.VMEM((2, biggest, biggest), jnp.float32),
            pltpu.VMEM((2, biggest, biggest), jnp.bfloat16),
            pltpu.VMEM((rows, SECTION), jnp.bfloat16),
            pltpu.VMEM((shards, rows // shards, width), jnp.bfloat16),
        ],
        compiler_params=limit(28),
    )(place, gathered, mod, w_qkv, w_out)


def regroup(first, second):
    low = lax.broadcasted_iota(jnp.int32, (8, 1), 0) < 4
    return (
        jnp.where(low, first, pltpu.roll(second, 4, 0)),
        jnp.where(low, pltpu.roll(first, 4, 0), second),
    )


def temporal_kernel(groups, group_of, mod_ref, w_ref, *refs):
    parts = 2 * CHIPS
    incoming, outgoing = arrived(refs[:parts]), sent(refs[parts : parts + CHIPS + 1])
    normed_ref, qkv_ref, s_ref, p_ref, mix_ref = refs[parts + CHIPS + 1 :]
    runs = refs[0].shape[0] // 8
    half = normed_ref.shape[0] // 2
    scale = 1.0 + mod_ref[4:5, :]
    shift = mod_ref[3:4, :]

    def run(place):
        return incoming[place // runs][place % runs * 8 : place % runs * 8 + 8]

    for at in range(0, half, 8):
        values = jnp.concatenate([run(at // 4), run(at // 4 + 1)], axis=0).astype(jnp.float32)
        center = values - jnp.mean(values, axis=-1, keepdims=True)
        spread = jnp.mean(center * center, axis=-1, keepdims=True)
        normed = center * lax.rsqrt(spread + EPS) * scale + shift
        for start, rows in zip((at, half + at), regroup(normed[:8], normed[8:])):
            normed_ref[start : start + 8] = rows.astype(jnp.bfloat16)
    project_qkv(normed_ref, w_ref, qkv_ref)
    mix_ref[...] = jnp.zeros_like(mix_ref)
    attend(groups, group_of, qkv_ref, s_ref, p_ref, mix_ref)
    for at in range(0, half, 8):
        low = mix_ref[at : at + 8, 0:HD].astype(jnp.float32)
        high = mix_ref[half + at : half + at + 8, 0:HD].astype(jnp.float32)
        for place, rows in zip((at // 4, at // 4 + 1), regroup(low, high)):
            b, start = place // runs, place % runs * 8
            outgoing[b // CHIPS * CHIPS + -b % CHIPS][start : start + 8] = rows.astype(jnp.bfloat16)


def temporal_block(parts, mod, w_qkv, groups, group_of):
    rows, width = parts[0].shape
    total = rows * len(parts)
    biggest = max(size for _, size in groups)
    return pl.pallas_call(
        functools.partial(temporal_kernel, groups, group_of),
        out_shape=sent_shapes(rows, HD, parts[0].dtype),
        in_specs=[VMEM] * (2 + len(parts)),
        out_specs=[VMEM] * (CHIPS + 1),
        scratch_shapes=[
            pltpu.VMEM((total, width), jnp.bfloat16),
            pltpu.VMEM((total, 3 * SECTION), jnp.bfloat16),
            pltpu.VMEM((2, biggest, biggest), jnp.float32),
            pltpu.VMEM((2, biggest, biggest), jnp.bfloat16),
            pltpu.VMEM((total, SECTION), jnp.bfloat16),
        ],
        compiler_params=limit(28),
    )(mod, w_qkv, *parts)


def final_kernel(place_ref, mod_ref, wo_ref, *refs):
    parts = 2 * CHIPS
    after_refs, mixed_refs = sent(refs[: CHIPS + 1]), arrived(refs[CHIPS + 1 : CHIPS + 1 + parts])
    o_hbm, all_ref, out_ref, sems = refs[CHIPS + 1 + parts :]
    rows = refs[0].shape[0]
    frame_count, widest = o_hbm.shape[0], o_hbm.shape[2]
    stores = []
    for half in range(2):
        for d in range(CHIPS):
            all_ref[half, d * rows : (d + 1) * rows] = mixed_refs[half * CHIPS + -d % CHIPS][...]
        projected = jnp.dot(all_ref[half], wo_ref[...], preferred_element_type=jnp.float32)
        core = place_ref[1] if half == 0 else 1 - place_ref[1]
        for d in range(CHIPS):
            part = half * CHIPS + d
            after = after_refs[part][...].astype(jnp.float32)
            result = (after + mod_ref[5:6, :] * projected[d * rows : (d + 1) * rows]).astype(jnp.bfloat16)
            for k in range(frame_count):
                out_ref[part, k] = result[k * widest : (k + 1) * widest]
            j = 2 * ((place_ref[0] + d) & (CHIPS - 1)) + core
            stores.append(pltpu.make_async_copy(out_ref.at[part], o_hbm.at[:, j], sems.at[part]))
            stores[-1].start()
    for store in stores:
        store.wait()


def final_block(place, mixed, after, mod, w_out):
    rows, width = after[0].shape
    parts = len(mixed)
    return pl.pallas_call(
        final_kernel,
        out_shape=jax.ShapeDtypeStruct((NFD, parts, rows // NFD, width), after[0].dtype),
        in_specs=[SMEM] + [VMEM] * (2 + len(after) + parts),
        out_specs=ANY,
        scratch_shapes=[
            pltpu.VMEM((2, CHIPS * rows, HD), jnp.bfloat16),
            pltpu.VMEM((parts, NFD, rows // NFD, width), jnp.bfloat16),
            pltpu.SemaphoreType.DMA((parts,)),
        ],
        compiler_params=limit(26),
    )(place, mod, w_out, *after, *mixed)


def exchange(near, crossing, *far):
    places = range(2 * CHIPS)

    def cross(part):
        return lax.ppermute(part, "seq", [(i, i ^ 1) for i in places])

    moved = [
        lax.ppermute(part, "seq", [(i, (i // 2 + d) % CHIPS * 2 + i % 2) for i in places])
        for d, part in enumerate(far, 1)
    ]
    return [near, *moved, cross(crossing), *(cross(part[1]) for part in moved)]


def source_index(counts, dest):
    groups, slots = dest.shape
    slot_ids = jnp.arange(slots, dtype=jnp.int32)
    live = slot_ids[None, :] < counts[:, None]
    targets = jnp.where(live, dest, -1).reshape(-1)
    wanted = jnp.arange(groups * NFD, dtype=jnp.int32)
    anchors = jnp.arange(groups * slots, dtype=jnp.int32)
    return jnp.sum(jnp.where(targets[None, :] == wanted[:, None], anchors[None, :], 0), axis=1)


def on_device(slot_tokens, modulation, counts, dest, qkv_spatial, out_spatial, qkv_temporal, out_temporal):
    groups = lax.axis_size("dp")
    shards = lax.axis_size("seq")
    slots, patches, width = slot_tokens.shape
    piece = patches // groups
    spread = lax.all_to_all(spread_pieces(slot_tokens, groups), "dp", split_axis=0, concat_axis=0, tiled=True)
    place = (lax.axis_index("seq") >> jnp.array([1, 0], jnp.int32)) & jnp.array([CHIPS - 1, 1], jnp.int32)
    spread, mod, index, place = lax.optimization_barrier(
        (spread, modulation[0], source_index(counts, dest), place)
    )
    chosen = choose_pieces(spread.reshape(groups * slots, piece, width), index)
    gathered = lax.all_to_all(
        chosen.reshape(groups, NFD, piece, width), "dp", split_axis=0, concat_axis=0, tiled=True
    )
    shift = patches.bit_length() - 1
    after = spatial_block(
        place,
        gathered,
        mod,
        qkv_spatial.T,
        out_spatial,
        ((0, 4 * patches), (4 * patches, 3 * patches)),
        lambda row: row >> shift,
        shards,
    )
    widest = patches // shards
    mixed = temporal_block(
        exchange(*after),
        mod,
        qkv_temporal.T,
        ((0, NFD * patches // 2), (NFD * patches // 2, NFD * patches // 2)),
        lambda row: row & (widest // 2 - 1),
    )
    return final_block(place, exchange(*mixed), after, mod, out_temporal).reshape(NFD, patches, width)


def solution(mesh):
    in_specs = (P("dp", "seq", None), P("dp", None, None), P(), P(), P(), P(), P(), P())
    return jax.shard_map(
        on_device, mesh=mesh, in_specs=in_specs, out_specs=P("dp", "seq", None), check_vma=False
    )
```

```python
import functools
import math

import jax
import jax.numpy as jnp
from jax import lax
from jax.experimental import pallas as pl
from jax.experimental.pallas import tpu as pltpu
from jax.sharding import PartitionSpec as P

HEADS = 8
HEAD_DIM = 72
HD = HEADS * HEAD_DIM
SECTION = 640
NFD = 7
EPS = 1e-06
LOW = -1e30
CHIPS = 4
ARRIVAL = (1, 3, 2)
NT = (((1,), (1,)), ((), ()))
VMEM = pl.BlockSpec(memory_space=pltpu.VMEM)
ANY = pl.BlockSpec(memory_space=pl.ANY)
SMEM = pl.BlockSpec(memory_space=pltpu.SMEM)


def limit(mib):
    return pltpu.CompilerParams(vmem_limit_bytes=mib * 1024 * 1024)


def spread_kernel(x_hbm, o_hbm, x_ref, o_ref, in_sems, out_sems):
    slots, patches, width = x_ref.shape
    groups = o_ref.shape[1]
    loads = [pltpu.make_async_copy(x_hbm.at[q], x_ref.at[q], in_sems.at[q]) for q in range(slots)]
    stores = [pltpu.make_async_copy(o_ref.at[q], o_hbm.at[:, q], out_sems.at[q]) for q in range(slots)]
    for load in loads:
        load.start()
    for q in range(slots):
        loads[q].wait()
        o_ref[q] = x_ref[q].reshape(groups, patches // groups, width)
        stores[q].start()
    for store in stores:
        store.wait()


def spread_pieces(slot_tokens, groups):
    slots, patches, width = slot_tokens.shape
    piece = patches // groups
    dtype = slot_tokens.dtype
    return pl.pallas_call(
        spread_kernel,
        out_shape=jax.ShapeDtypeStruct((groups, slots, piece, width), dtype),
        in_specs=[ANY],
        out_specs=ANY,
        scratch_shapes=[
            pltpu.VMEM((slots, patches, width), dtype),
            pltpu.VMEM((slots, groups, piece, width), dtype),
            pltpu.SemaphoreType.DMA((slots,)),
            pltpu.SemaphoreType.DMA((slots,)),
        ],
        compiler_params=limit(63),
    )(slot_tokens)


def choose_kernel(index_ref, x_ref, o_ref):
    unroll = 8

    def body(i, carry):
        for j in range(unroll):
            o_ref[i * unroll + j] = x_ref[index_ref[i * unroll + j]]
        return carry

    lax.fori_loop(0, o_ref.shape[0] // unroll, body, 0)


def choose_pieces(spread, index):
    return pl.pallas_call(
        choose_kernel,
        out_shape=jax.ShapeDtypeStruct((index.shape[0],) + spread.shape[1:], spread.dtype),
        in_specs=[SMEM, VMEM],
        out_specs=VMEM,
        compiler_params=limit(26),
    )(index, spread)


def normalize(load, mod_ref, base, normed_ref):
    total = normed_ref.shape[0]
    scale = 1.0 + mod_ref[base + 1 : base + 2, :]
    shift = mod_ref[base : base + 1, :]
    for at in range(0, total, 16):
        step = min(16, total - at)
        values = load(at, step).astype(jnp.float32)
        center = values - jnp.mean(values, axis=-1, keepdims=True)
        spread = jnp.mean(center * center, axis=-1, keepdims=True)
        normed_ref[at : at + step] = (center * lax.rsqrt(spread + EPS) * scale + shift).astype(jnp.bfloat16)


def project_qkv(normed_ref, w_ref, qkv_ref):
    normed = normed_ref[...]
    for part in range(3):
        start = part * SECTION
        qkv_ref[:, start + SECTION - 128 : start + SECTION] = jnp.zeros((normed.shape[0], 128), jnp.bfloat16)
    rows = normed.shape[0] // 2
    for at in range(0, 2 * rows, rows):
        full = lax.dot_general(normed[at : at + rows], w_ref[...], NT, preferred_element_type=jnp.float32)
        for part in range(3):
            qkv_ref[at : at + rows, part * SECTION : part * SECTION + HD] = full[
                :, part * HD : (part + 1) * HD
            ].astype(jnp.bfloat16)


def attend(groups, group_of, qkv_ref, s_ref, p_ref, mix_ref):
    factor = math.log2(math.e) / math.sqrt(HEAD_DIM)
    lane = lax.broadcasted_iota(jnp.int32, (1, 256), 1)
    tasks = [(h, start, size) for start, size in groups for h in range(HEADS)]

    def window(h):
        base = (HEAD_DIM * h) // 128 * 128
        low = HEAD_DIM * h - base
        return base, (lane >= low) & (lane < low + HEAD_DIM)

    def scores(t):
        h, start, size = tasks[t]
        base, own = window(h)
        rows = pl.ds(start, size)
        q = jnp.where(own, qkv_ref[rows, pl.ds(base, 256)], jnp.bfloat16(0))
        k = qkv_ref[rows, pl.ds(SECTION + base, 256)]
        s_ref[t % 2, :size, :size] = lax.dot_general(q, k, NT, preferred_element_type=jnp.float32)

    def weights(t):
        h, start, size = tasks[t]
        same = group_of(lax.broadcasted_iota(jnp.int32, (size, 1), 0)) == group_of(
            lax.broadcasted_iota(jnp.int32, (1, size), 1)
        )
        s = jnp.where(same, s_ref[t % 2, :size, :size], LOW)
        raised = jnp.exp2((s - jnp.max(s, axis=-1, keepdims=True)) * factor)
        inverse = 1.0 / jnp.sum(raised, axis=-1, keepdims=True)
        p_ref[t % 2, :size, :size] = (raised * inverse).astype(jnp.bfloat16)

    def mixing(t):
        h, start, size = tasks[t]
        base, own = window(h)
        rows = pl.ds(start, size)
        mixed = jnp.dot(
            p_ref[t % 2, :size, :size],
            qkv_ref[rows, pl.ds(2 * SECTION + base, 256)],
            preferred_element_type=jnp.float32,
        ).astype(jnp.bfloat16)
        mix_ref[rows, pl.ds(base, 256)] = jnp.where(own, mixed, mix_ref[rows, pl.ds(base, 256)])

    scores(0)
    for t in range(len(tasks)):
        if t + 1 < len(tasks):
            scores(t + 1)
        weights(t)
        mixing(t)


def sent(refs):
    far = refs[2:]
    return [refs[0]] + [ref.at[0] for ref in far] + [refs[1]] + [ref.at[1] for ref in far]


def sent_shapes(rows, width, dtype):
    near, far = jax.ShapeDtypeStruct((rows, width), dtype), jax.ShapeDtypeStruct((2, rows, width), dtype)
    return [near] * 2 + [far] * (CHIPS - 1)


def arrived(refs):
    crossed, near, moved = refs[:CHIPS], refs[CHIPS], refs[CHIPS + 1 :]
    parts = {0: near, CHIPS: crossed[0]}
    for place, d in enumerate(ARRIVAL):
        parts[d] = moved[place].at[0]
        parts[CHIPS + d] = crossed[1 + place]
    return [parts[part] for part in range(2 * CHIPS)]


def spatial_kernel(
    groups, group_of, place_ref, x_ref, mod_ref, w_ref, wo_ref, *refs
):
    o_refs, (frames_ref, normed_ref, qkv_ref, s_ref, p_ref, mix_ref, after_ref) = refs[: CHIPS + 1], refs[CHIPS + 1 :]
    outgoing = sent(o_refs)
    frame_count = x_ref.shape[1]
    patches = frames_ref.shape[0] // frame_count

    def load(at, step):
        k, w = at // patches, at % patches // 2
        rows = x_ref[w : w + step // 2, k].reshape(step, x_ref.shape[3])
        frames_ref[at : at + step] = rows
        return rows

    normalize(load, mod_ref, 0, normed_ref)
    project_qkv(normed_ref, w_ref, qkv_ref)
    mix_ref[...] = jnp.zeros_like(mix_ref)
    attend(groups, group_of, qkv_ref, s_ref, p_ref, mix_ref)
    shards = after_ref.shape[0]
    widest = patches // shards
    for start, size in groups:
        rows = pl.ds(start, size)
        projected = jnp.dot(mix_ref[rows, 0:HD], wo_ref[...], preferred_element_type=jnp.float32)
        after = (frames_ref[rows, :].astype(jnp.float32) + mod_ref[2:3, :] * projected).astype(jnp.bfloat16)
        for at in range(0, size, widest):
            k, j = (start + at) // patches, (start + at) % patches // widest
            after_ref[j, k * widest : (k + 1) * widest, :] = after[at : at + widest]
    for d in range(CHIPS):
        chip = 2 * ((place_ref[0] + d) & (CHIPS - 1))
        outgoing[d][...] = after_ref[chip + place_ref[1]]
        outgoing[CHIPS + d][...] = after_ref[chip + 1 - place_ref[1]]


def spatial_block(place, gathered, mod, w_qkv, w_out, groups, group_of, shards):
    pieces, frame_count, piece, width = gathered.shape
    rows = pieces * frame_count * piece
    biggest = max(size for _, size in groups)
    return pl.pallas_call(
        functools.partial(spatial_kernel, groups, group_of),
        out_shape=sent_shapes(rows // shards, width, gathered.dtype),
        in_specs=[SMEM] + [VMEM] * 4,
        out_specs=[VMEM] * (CHIPS + 1),
        scratch_shapes=[
            pltpu.VMEM((rows, width), jnp.bfloat16),
            pltpu.VMEM((rows, width), jnp.bfloat16),
            pltpu.VMEM((rows, 3 * SECTION), jnp.bfloat16),
            pltpu.VMEM((2, biggest, biggest), jnp.float32),
            pltpu.VMEM((2, biggest, biggest), jnp.bfloat16),
            pltpu.VMEM((rows, SECTION), jnp.bfloat16),
            pltpu.VMEM((shards, rows // shards, width), jnp.bfloat16),
        ],
        compiler_params=limit(28),
    )(place, gathered, mod, w_qkv, w_out)


def regroup(first, second):
    low = lax.broadcasted_iota(jnp.int32, (8, 1), 0) < 4
    return (
        jnp.where(low, first, pltpu.roll(second, 4, 0)),
        jnp.where(low, pltpu.roll(first, 4, 0), second),
    )


def temporal_kernel(groups, group_of, mod_ref, w_ref, *refs):
    parts = 2 * CHIPS
    incoming, outgoing = arrived(refs[:parts]), sent(refs[parts : parts + CHIPS + 1])
    normed_ref, qkv_ref, s_ref, p_ref, mix_ref = refs[parts + CHIPS + 1 :]
    runs = refs[0].shape[0] // 8
    half = normed_ref.shape[0] // 2
    scale = 1.0 + mod_ref[4:5, :]
    shift = mod_ref[3:4, :]

    def run(place):
        return incoming[place // runs][place % runs * 8 : place % runs * 8 + 8]

    for at in range(0, half, 8):
        values = jnp.concatenate([run(at // 4), run(at // 4 + 1)], axis=0).astype(jnp.float32)
        center = values - jnp.mean(values, axis=-1, keepdims=True)
        spread = jnp.mean(center * center, axis=-1, keepdims=True)
        normed = center * lax.rsqrt(spread + EPS) * scale + shift
        for start, rows in zip((at, half + at), regroup(normed[:8], normed[8:])):
            normed_ref[start : start + 8] = rows.astype(jnp.bfloat16)
    project_qkv(normed_ref, w_ref, qkv_ref)
    mix_ref[...] = jnp.zeros_like(mix_ref)
    attend(groups, group_of, qkv_ref, s_ref, p_ref, mix_ref)
    for at in range(0, half, 8):
        low = mix_ref[at : at + 8, 0:HD].astype(jnp.float32)
        high = mix_ref[half + at : half + at + 8, 0:HD].astype(jnp.float32)
        for place, rows in zip((at // 4, at // 4 + 1), regroup(low, high)):
            b, start = place // runs, place % runs * 8
            outgoing[b // CHIPS * CHIPS + -b % CHIPS][start : start + 8] = rows.astype(jnp.bfloat16)


def temporal_block(parts, mod, w_qkv, groups, group_of):
    rows, width = parts[0].shape
    total = rows * len(parts)
    biggest = max(size for _, size in groups)
    return pl.pallas_call(
        functools.partial(temporal_kernel, groups, group_of),
        out_shape=sent_shapes(rows, HD, parts[0].dtype),
        in_specs=[VMEM] * (2 + len(parts)),
        out_specs=[VMEM] * (CHIPS + 1),
        scratch_shapes=[
            pltpu.VMEM((total, width), jnp.bfloat16),
            pltpu.VMEM((total, 3 * SECTION), jnp.bfloat16),
            pltpu.VMEM((2, biggest, biggest), jnp.float32),
            pltpu.VMEM((2, biggest, biggest), jnp.bfloat16),
            pltpu.VMEM((total, SECTION), jnp.bfloat16),
        ],
        compiler_params=limit(28),
    )(mod, w_qkv, *parts)


def final_kernel(place_ref, mod_ref, wo_ref, *refs):
    parts = 2 * CHIPS
    after_refs, mixed_refs = sent(refs[: CHIPS + 1]), arrived(refs[CHIPS + 1 : CHIPS + 1 + parts])
    o_hbm, all_ref, out_ref, sems = refs[CHIPS + 1 + parts :]
    rows = refs[0].shape[0]
    frame_count, widest = o_hbm.shape[0], o_hbm.shape[2]
    stores = []
    for half in range(2):
        for d in range(CHIPS):
            all_ref[half, d * rows : (d + 1) * rows] = mixed_refs[half * CHIPS + -d % CHIPS][...]
        projected = jnp.dot(all_ref[half], wo_ref[...], preferred_element_type=jnp.float32)
        core = place_ref[1] if half == 0 else 1 - place_ref[1]
        for d in range(CHIPS):
            part = half * CHIPS + d
            after = after_refs[part][...].astype(jnp.float32)
            result = (after + mod_ref[5:6, :] * projected[d * rows : (d + 1) * rows]).astype(jnp.bfloat16)
            for k in range(frame_count):
                out_ref[part, k] = result[k * widest : (k + 1) * widest]
            j = 2 * ((place_ref[0] + d) & (CHIPS - 1)) + core
            stores.append(pltpu.make_async_copy(out_ref.at[part], o_hbm.at[:, j], sems.at[part]))
            stores[-1].start()
    for store in stores:
        store.wait()


def final_block(place, mixed, after, mod, w_out):
    rows, width = after[0].shape
    parts = len(mixed)
    return pl.pallas_call(
        final_kernel,
        out_shape=jax.ShapeDtypeStruct((NFD, parts, rows // NFD, width), after[0].dtype),
        in_specs=[SMEM] + [VMEM] * (2 + len(after) + parts),
        out_specs=ANY,
        scratch_shapes=[
            pltpu.VMEM((2, CHIPS * rows, HD), jnp.bfloat16),
            pltpu.VMEM((parts, NFD, rows // NFD, width), jnp.bfloat16),
            pltpu.SemaphoreType.DMA((parts,)),
        ],
        compiler_params=limit(26),
    )(place, mod, w_out, *after, *mixed)


def exchange(near, crossing, *far):
    places = range(2 * CHIPS)

    def cross(part):
        return lax.ppermute(part, "seq", [(i, i ^ 1) for i in places])

    moved = [
        lax.ppermute(far[d - 1], "seq", [(i, (i // 2 + d) % CHIPS * 2 + i % 2) for i in places])
        for d in ARRIVAL
    ]
    return [cross(crossing), *(cross(part[1]) for part in moved), near, *moved]


def source_index(counts, dest):
    groups, slots = dest.shape
    slot_ids = jnp.arange(slots, dtype=jnp.int32)
    live = slot_ids[None, :] < counts[:, None]
    targets = jnp.where(live, dest, -1).reshape(-1)
    wanted = jnp.arange(groups * NFD, dtype=jnp.int32)
    anchors = jnp.arange(groups * slots, dtype=jnp.int32)
    return jnp.sum(jnp.where(targets[None, :] == wanted[:, None], anchors[None, :], 0), axis=1)


def on_device(slot_tokens, modulation, counts, dest, qkv_spatial, out_spatial, qkv_temporal, out_temporal):
    groups = lax.axis_size("dp")
    shards = lax.axis_size("seq")
    slots, patches, width = slot_tokens.shape
    piece = patches // groups
    spread = lax.all_to_all(spread_pieces(slot_tokens, groups), "dp", split_axis=0, concat_axis=0, tiled=True)
    place = (lax.axis_index("seq") >> jnp.array([1, 0], jnp.int32)) & jnp.array([CHIPS - 1, 1], jnp.int32)
    spread, mod, index, place = lax.optimization_barrier(
        (spread, modulation[0], source_index(counts, dest), place)
    )
    chosen = choose_pieces(spread.reshape(groups * slots, piece, width), index)
    gathered = lax.all_to_all(
        chosen.reshape(groups, NFD, piece, width), "dp", split_axis=0, concat_axis=0, tiled=True
    )
    shift = patches.bit_length() - 1
    after = spatial_block(
        place,
        gathered,
        mod,
        qkv_spatial.T,
        out_spatial,
        ((0, 4 * patches), (4 * patches, 3 * patches)),
        lambda row: row >> shift,
        shards,
    )
    widest = patches // shards
    mixed = temporal_block(
        exchange(*after),
        mod,
        qkv_temporal.T,
        ((0, NFD * patches // 2), (NFD * patches // 2, NFD * patches // 2)),
        lambda row: row & (widest // 2 - 1),
    )
    return final_block(place, exchange(*mixed), after, mod, out_temporal).reshape(NFD, patches, width)


def solution(mesh):
    in_specs = (P("dp", "seq", None), P("dp", None, None), P(), P(), P(), P(), P(), P())
    return jax.shard_map(
        on_device, mesh=mesh, in_specs=in_specs, out_specs=P("dp", "seq", None), check_vma=False
    )
```

```python
import functools
import math

import jax
import jax.numpy as jnp
from jax import lax
from jax.experimental import pallas as pl
from jax.experimental.pallas import tpu as pltpu
from jax.sharding import PartitionSpec as P

HEADS = 8
HEAD_DIM = 72
HD = HEADS * HEAD_DIM
SECTION = 640
NFD = 7
EPS = 1e-06
LOW = -1e30
CHIPS = 4
ARRIVAL = (2, 1, 3)
NT = (((1,), (1,)), ((), ()))
VMEM = pl.BlockSpec(memory_space=pltpu.VMEM)
ANY = pl.BlockSpec(memory_space=pl.ANY)
SMEM = pl.BlockSpec(memory_space=pltpu.SMEM)


def limit(mib):
    return pltpu.CompilerParams(vmem_limit_bytes=mib * 1024 * 1024)


def spread_kernel(x_hbm, o_hbm, x_ref, o_ref, in_sems, out_sems):
    slots, patches, width = x_ref.shape
    groups = o_ref.shape[1]
    loads = [pltpu.make_async_copy(x_hbm.at[q], x_ref.at[q], in_sems.at[q]) for q in range(slots)]
    stores = [pltpu.make_async_copy(o_ref.at[q], o_hbm.at[:, q], out_sems.at[q]) for q in range(slots)]
    for load in loads:
        load.start()
    for q in range(slots):
        loads[q].wait()
        o_ref[q] = x_ref[q].reshape(groups, patches // groups, width)
        stores[q].start()
    for store in stores:
        store.wait()


def spread_pieces(slot_tokens, groups):
    slots, patches, width = slot_tokens.shape
    piece = patches // groups
    dtype = slot_tokens.dtype
    return pl.pallas_call(
        spread_kernel,
        out_shape=jax.ShapeDtypeStruct((groups, slots, piece, width), dtype),
        in_specs=[ANY],
        out_specs=ANY,
        scratch_shapes=[
            pltpu.VMEM((slots, patches, width), dtype),
            pltpu.VMEM((slots, groups, piece, width), dtype),
            pltpu.SemaphoreType.DMA((slots,)),
            pltpu.SemaphoreType.DMA((slots,)),
        ],
        compiler_params=limit(63),
    )(slot_tokens)


def choose_kernel(index_ref, x_ref, o_ref):
    unroll = 8

    def body(i, carry):
        for j in range(unroll):
            o_ref[i * unroll + j] = x_ref[index_ref[i * unroll + j]]
        return carry

    lax.fori_loop(0, o_ref.shape[0] // unroll, body, 0)


def choose_pieces(spread, index):
    return pl.pallas_call(
        choose_kernel,
        out_shape=jax.ShapeDtypeStruct((index.shape[0],) + spread.shape[1:], spread.dtype),
        in_specs=[SMEM, VMEM],
        out_specs=VMEM,
        compiler_params=limit(26),
    )(index, spread)


def normalize(load, mod_ref, base, normed_ref):
    total = normed_ref.shape[0]
    scale = 1.0 + mod_ref[base + 1 : base + 2, :]
    shift = mod_ref[base : base + 1, :]
    for at in range(0, total, 16):
        step = min(16, total - at)
        values = load(at, step).astype(jnp.float32)
        center = values - jnp.mean(values, axis=-1, keepdims=True)
        spread = jnp.mean(center * center, axis=-1, keepdims=True)
        normed_ref[at : at + step] = (center * lax.rsqrt(spread + EPS) * scale + shift).astype(jnp.bfloat16)


def project_qkv(normed_ref, w_ref, qkv_ref):
    normed = normed_ref[...]
    for part in range(3):
        start = part * SECTION
        qkv_ref[:, start + SECTION - 128 : start + SECTION] = jnp.zeros((normed.shape[0], 128), jnp.bfloat16)
    rows = normed.shape[0] // 2
    for at in range(0, 2 * rows, rows):
        full = lax.dot_general(normed[at : at + rows], w_ref[...], NT, preferred_element_type=jnp.float32)
        for part in range(3):
            qkv_ref[at : at + rows, part * SECTION : part * SECTION + HD] = full[
                :, part * HD : (part + 1) * HD
            ].astype(jnp.bfloat16)


def attend(groups, group_of, qkv_ref, s_ref, p_ref, mix_ref):
    factor = math.log2(math.e) / math.sqrt(HEAD_DIM)
    lane = lax.broadcasted_iota(jnp.int32, (1, 256), 1)
    tasks = [(h, start, size) for start, size in groups for h in range(HEADS)]

    def window(h):
        base = (HEAD_DIM * h) // 128 * 128
        low = HEAD_DIM * h - base
        return base, (lane >= low) & (lane < low + HEAD_DIM)

    def scores(t):
        h, start, size = tasks[t]
        base, own = window(h)
        rows = pl.ds(start, size)
        q = jnp.where(own, qkv_ref[rows, pl.ds(base, 256)], jnp.bfloat16(0))
        k = qkv_ref[rows, pl.ds(SECTION + base, 256)]
        s_ref[t % 2, :size, :size] = lax.dot_general(q, k, NT, preferred_element_type=jnp.float32)

    def weights(t):
        h, start, size = tasks[t]
        same = group_of(lax.broadcasted_iota(jnp.int32, (size, 1), 0)) == group_of(
            lax.broadcasted_iota(jnp.int32, (1, size), 1)
        )
        s = jnp.where(same, s_ref[t % 2, :size, :size], LOW)
        raised = jnp.exp2((s - jnp.max(s, axis=-1, keepdims=True)) * factor)
        inverse = 1.0 / jnp.sum(raised, axis=-1, keepdims=True)
        p_ref[t % 2, :size, :size] = (raised * inverse).astype(jnp.bfloat16)

    def mixing(t):
        h, start, size = tasks[t]
        base, own = window(h)
        rows = pl.ds(start, size)
        mixed = jnp.dot(
            p_ref[t % 2, :size, :size],
            qkv_ref[rows, pl.ds(2 * SECTION + base, 256)],
            preferred_element_type=jnp.float32,
        ).astype(jnp.bfloat16)
        mix_ref[rows, pl.ds(base, 256)] = jnp.where(own, mixed, mix_ref[rows, pl.ds(base, 256)])

    scores(0)
    for t in range(len(tasks)):
        if t + 1 < len(tasks):
            scores(t + 1)
        weights(t)
        mixing(t)


def sent(refs):
    far = refs[2:]
    return [refs[0]] + [ref.at[0] for ref in far] + [refs[1]] + [ref.at[1] for ref in far]


def sent_shapes(rows, width, dtype):
    near, far = jax.ShapeDtypeStruct((rows, width), dtype), jax.ShapeDtypeStruct((2, rows, width), dtype)
    return [near] * 2 + [far] * (CHIPS - 1)


def arrived(refs):
    crossed, near, moved = refs[:CHIPS], refs[CHIPS], refs[CHIPS + 1 :]
    parts = {0: near, CHIPS: crossed[0]}
    for place, d in enumerate(ARRIVAL):
        parts[d] = moved[place].at[0]
        parts[CHIPS + d] = crossed[1 + place]
    return [parts[part] for part in range(2 * CHIPS)]


def spatial_kernel(
    groups, group_of, place_ref, x_ref, mod_ref, w_ref, wo_ref, *refs
):
    o_refs, (frames_ref, normed_ref, qkv_ref, s_ref, p_ref, mix_ref, after_ref) = refs[: CHIPS + 1], refs[CHIPS + 1 :]
    outgoing = sent(o_refs)
    frame_count = x_ref.shape[1]
    patches = frames_ref.shape[0] // frame_count

    def load(at, step):
        k, w = at // patches, at % patches // 2
        rows = x_ref[w : w + step // 2, k].reshape(step, x_ref.shape[3])
        frames_ref[at : at + step] = rows
        return rows

    normalize(load, mod_ref, 0, normed_ref)
    project_qkv(normed_ref, w_ref, qkv_ref)
    mix_ref[...] = jnp.zeros_like(mix_ref)
    attend(groups, group_of, qkv_ref, s_ref, p_ref, mix_ref)
    shards = after_ref.shape[0]
    widest = patches // shards
    for start, size in groups:
        rows = pl.ds(start, size)
        projected = jnp.dot(mix_ref[rows, 0:HD], wo_ref[...], preferred_element_type=jnp.float32)
        after = (frames_ref[rows, :].astype(jnp.float32) + mod_ref[2:3, :] * projected).astype(jnp.bfloat16)
        for at in range(0, size, widest):
            k, j = (start + at) // patches, (start + at) % patches // widest
            after_ref[j, k * widest : (k + 1) * widest, :] = after[at : at + widest]
    for d in range(CHIPS):
        chip = 2 * ((place_ref[0] + d) & (CHIPS - 1))
        outgoing[d][...] = after_ref[chip + place_ref[1]]
        outgoing[CHIPS + d][...] = after_ref[chip + 1 - place_ref[1]]


def spatial_block(place, gathered, mod, w_qkv, w_out, groups, group_of, shards):
    pieces, frame_count, piece, width = gathered.shape
    rows = pieces * frame_count * piece
    biggest = max(size for _, size in groups)
    return pl.pallas_call(
        functools.partial(spatial_kernel, groups, group_of),
        out_shape=sent_shapes(rows // shards, width, gathered.dtype),
        in_specs=[SMEM] + [VMEM] * 4,
        out_specs=[VMEM] * (CHIPS + 1),
        scratch_shapes=[
            pltpu.VMEM((rows, width), jnp.bfloat16),
            pltpu.VMEM((rows, width), jnp.bfloat16),
            pltpu.VMEM((rows, 3 * SECTION), jnp.bfloat16),
            pltpu.VMEM((2, biggest, biggest), jnp.float32),
            pltpu.VMEM((2, biggest, biggest), jnp.bfloat16),
            pltpu.VMEM((rows, SECTION), jnp.bfloat16),
            pltpu.VMEM((shards, rows // shards, width), jnp.bfloat16),
        ],
        compiler_params=limit(28),
    )(place, gathered, mod, w_qkv, w_out)


def regroup(first, second):
    low = lax.broadcasted_iota(jnp.int32, (8, 1), 0) < 4
    return (
        jnp.where(low, first, pltpu.roll(second, 4, 0)),
        jnp.where(low, pltpu.roll(first, 4, 0), second),
    )


def temporal_kernel(groups, group_of, mod_ref, w_ref, *refs):
    parts = 2 * CHIPS
    incoming, outgoing = arrived(refs[:parts]), sent(refs[parts : parts + CHIPS + 1])
    normed_ref, qkv_ref, s_ref, p_ref, mix_ref = refs[parts + CHIPS + 1 :]
    runs = refs[0].shape[0] // 8
    half = normed_ref.shape[0] // 2
    scale = 1.0 + mod_ref[4:5, :]
    shift = mod_ref[3:4, :]

    def run(place):
        return incoming[place // runs][place % runs * 8 : place % runs * 8 + 8]

    for at in range(0, half, 8):
        values = jnp.concatenate([run(at // 4), run(at // 4 + 1)], axis=0).astype(jnp.float32)
        center = values - jnp.mean(values, axis=-1, keepdims=True)
        spread = jnp.mean(center * center, axis=-1, keepdims=True)
        normed = center * lax.rsqrt(spread + EPS) * scale + shift
        for start, rows in zip((at, half + at), regroup(normed[:8], normed[8:])):
            normed_ref[start : start + 8] = rows.astype(jnp.bfloat16)
    project_qkv(normed_ref, w_ref, qkv_ref)
    mix_ref[...] = jnp.zeros_like(mix_ref)
    attend(groups, group_of, qkv_ref, s_ref, p_ref, mix_ref)
    for at in range(0, half, 8):
        low = mix_ref[at : at + 8, 0:HD].astype(jnp.float32)
        high = mix_ref[half + at : half + at + 8, 0:HD].astype(jnp.float32)
        for place, rows in zip((at // 4, at // 4 + 1), regroup(low, high)):
            b, start = place // runs, place % runs * 8
            outgoing[b // CHIPS * CHIPS + -b % CHIPS][start : start + 8] = rows.astype(jnp.bfloat16)


def temporal_block(parts, mod, w_qkv, groups, group_of):
    rows, width = parts[0].shape
    total = rows * len(parts)
    biggest = max(size for _, size in groups)
    return pl.pallas_call(
        functools.partial(temporal_kernel, groups, group_of),
        out_shape=sent_shapes(rows, HD, parts[0].dtype),
        in_specs=[VMEM] * (2 + len(parts)),
        out_specs=[VMEM] * (CHIPS + 1),
        scratch_shapes=[
            pltpu.VMEM((total, width), jnp.bfloat16),
            pltpu.VMEM((total, 3 * SECTION), jnp.bfloat16),
            pltpu.VMEM((2, biggest, biggest), jnp.float32),
            pltpu.VMEM((2, biggest, biggest), jnp.bfloat16),
            pltpu.VMEM((total, SECTION), jnp.bfloat16),
        ],
        compiler_params=limit(28),
    )(mod, w_qkv, *parts)


def final_kernel(place_ref, mod_ref, wo_ref, *refs):
    parts = 2 * CHIPS
    after_refs, mixed_refs = sent(refs[: CHIPS + 1]), arrived(refs[CHIPS + 1 : CHIPS + 1 + parts])
    o_hbm, all_ref, out_ref, sems = refs[CHIPS + 1 + parts :]
    rows = refs[0].shape[0]
    frame_count, widest = o_hbm.shape[0], o_hbm.shape[2]
    stores = []
    for half in range(2):
        for d in range(CHIPS):
            all_ref[half, d * rows : (d + 1) * rows] = mixed_refs[half * CHIPS + -d % CHIPS][...]
        projected = jnp.dot(all_ref[half], wo_ref[...], preferred_element_type=jnp.float32)
        core = place_ref[1] if half == 0 else 1 - place_ref[1]
        for d in range(CHIPS):
            part = half * CHIPS + d
            after = after_refs[part][...].astype(jnp.float32)
            result = (after + mod_ref[5:6, :] * projected[d * rows : (d + 1) * rows]).astype(jnp.bfloat16)
            for k in range(frame_count):
                out_ref[part, k] = result[k * widest : (k + 1) * widest]
            j = 2 * ((place_ref[0] + d) & (CHIPS - 1)) + core
            stores.append(pltpu.make_async_copy(out_ref.at[part], o_hbm.at[:, j], sems.at[part]))
            stores[-1].start()
    for store in stores:
        store.wait()


def final_block(place, mixed, after, mod, w_out):
    rows, width = after[0].shape
    parts = len(mixed)
    return pl.pallas_call(
        final_kernel,
        out_shape=jax.ShapeDtypeStruct((NFD, parts, rows // NFD, width), after[0].dtype),
        in_specs=[SMEM] + [VMEM] * (2 + len(after) + parts),
        out_specs=ANY,
        scratch_shapes=[
            pltpu.VMEM((2, CHIPS * rows, HD), jnp.bfloat16),
            pltpu.VMEM((parts, NFD, rows // NFD, width), jnp.bfloat16),
            pltpu.SemaphoreType.DMA((parts,)),
        ],
        compiler_params=limit(26),
    )(place, mod, w_out, *after, *mixed)


def exchange(near, crossing, *far):
    places = range(2 * CHIPS)

    def cross(part):
        return lax.ppermute(part, "seq", [(i, i ^ 1) for i in places])

    moved = [
        lax.ppermute(far[d - 1], "seq", [(i, (i // 2 + d) % CHIPS * 2 + i % 2) for i in places])
        for d in ARRIVAL
    ]
    return [cross(crossing), *(cross(part[1]) for part in moved), near, *moved]


def source_index(counts, dest):
    groups, slots = dest.shape
    slot_ids = jnp.arange(slots, dtype=jnp.int32)
    live = slot_ids[None, :] < counts[:, None]
    targets = jnp.where(live, dest, -1).reshape(-1)
    wanted = jnp.arange(groups * NFD, dtype=jnp.int32)
    anchors = jnp.arange(groups * slots, dtype=jnp.int32)
    return jnp.sum(jnp.where(targets[None, :] == wanted[:, None], anchors[None, :], 0), axis=1)


def on_device(slot_tokens, modulation, counts, dest, qkv_spatial, out_spatial, qkv_temporal, out_temporal):
    groups = lax.axis_size("dp")
    shards = lax.axis_size("seq")
    slots, patches, width = slot_tokens.shape
    piece = patches // groups
    spread = lax.all_to_all(spread_pieces(slot_tokens, groups), "dp", split_axis=0, concat_axis=0, tiled=True)
    place = (lax.axis_index("seq") >> jnp.array([1, 0], jnp.int32)) & jnp.array([CHIPS - 1, 1], jnp.int32)
    spread, mod, index, place = lax.optimization_barrier(
        (spread, modulation[0], source_index(counts, dest), place)
    )
    chosen = choose_pieces(spread.reshape(groups * slots, piece, width), index)
    gathered = lax.all_to_all(
        chosen.reshape(groups, NFD, piece, width), "dp", split_axis=0, concat_axis=0, tiled=True
    )
    shift = patches.bit_length() - 1
    after = spatial_block(
        place,
        gathered,
        mod,
        qkv_spatial.T,
        out_spatial,
        ((0, 4 * patches), (4 * patches, 3 * patches)),
        lambda row: row >> shift,
        shards,
    )
    widest = patches // shards
    mixed = temporal_block(
        exchange(*after),
        mod,
        qkv_temporal.T,
        ((0, NFD * patches // 2), (NFD * patches // 2, NFD * patches // 2)),
        lambda row: row & (widest // 2 - 1),
    )
    return final_block(place, exchange(*mixed), after, mod, out_temporal).reshape(NFD, patches, width)


def solution(mesh):
    in_specs = (P("dp", "seq", None), P("dp", None, None), P(), P(), P(), P(), P(), P())
    return jax.shard_map(
        on_device, mesh=mesh, in_specs=in_specs, out_specs=P("dp", "seq", None), check_vma=False
    )
```

```python
import functools
import math

import jax
import jax.numpy as jnp
from jax import lax
from jax.experimental import pallas as pl
from jax.experimental.pallas import tpu as pltpu
from jax.sharding import PartitionSpec as P

HEADS = 8
HEAD_DIM = 72
HD = HEADS * HEAD_DIM
SECTION = 640
NFD = 7
EPS = 1e-06
LOW = -1e30
CHIPS = 4
ARRIVAL = (2, 1, 3)
NT = (((1,), (1,)), ((), ()))
VMEM = pl.BlockSpec(memory_space=pltpu.VMEM)
ANY = pl.BlockSpec(memory_space=pl.ANY)
SMEM = pl.BlockSpec(memory_space=pltpu.SMEM)


def limit(mib):
    return pltpu.CompilerParams(vmem_limit_bytes=mib * 1024 * 1024)


def spread_kernel(x_hbm, o_hbm, x_ref, o_ref, in_sems, out_sems):
    slots, patches, width = x_ref.shape
    groups = o_ref.shape[1]
    loads = [pltpu.make_async_copy(x_hbm.at[q], x_ref.at[q], in_sems.at[q]) for q in range(slots)]
    stores = [pltpu.make_async_copy(o_ref.at[q], o_hbm.at[:, q], out_sems.at[q]) for q in range(slots)]
    for load in loads:
        load.start()
    for q in range(slots):
        loads[q].wait()
        o_ref[q] = x_ref[q].reshape(groups, patches // groups, width)
        stores[q].start()
    for store in stores:
        store.wait()


def spread_pieces(slot_tokens, groups):
    slots, patches, width = slot_tokens.shape
    piece = patches // groups
    dtype = slot_tokens.dtype
    return pl.pallas_call(
        spread_kernel,
        out_shape=jax.ShapeDtypeStruct((groups, slots, piece, width), dtype),
        in_specs=[ANY],
        out_specs=ANY,
        scratch_shapes=[
            pltpu.VMEM((slots, patches, width), dtype),
            pltpu.VMEM((slots, groups, piece, width), dtype),
            pltpu.SemaphoreType.DMA((slots,)),
            pltpu.SemaphoreType.DMA((slots,)),
        ],
        compiler_params=limit(63),
    )(slot_tokens)


def choose_kernel(index_ref, x_ref, o_ref):
    unroll = 8

    def body(i, carry):
        for j in range(unroll):
            o_ref[i * unroll + j] = x_ref[index_ref[i * unroll + j]]
        return carry

    lax.fori_loop(0, o_ref.shape[0] // unroll, body, 0)


def choose_pieces(spread, index):
    return pl.pallas_call(
        choose_kernel,
        out_shape=jax.ShapeDtypeStruct((index.shape[0],) + spread.shape[1:], spread.dtype),
        in_specs=[SMEM, VMEM],
        out_specs=VMEM,
        compiler_params=limit(26),
    )(index, spread)


def normalize(load, mod_ref, base, normed_ref):
    total = normed_ref.shape[0]
    scale = 1.0 + mod_ref[base + 1 : base + 2, :]
    shift = mod_ref[base : base + 1, :]
    for at in range(0, total, 16):
        step = min(16, total - at)
        values = load(at, step).astype(jnp.float32)
        center = values - jnp.mean(values, axis=-1, keepdims=True)
        spread = jnp.mean(center * center, axis=-1, keepdims=True)
        normed_ref[at : at + step] = (center * lax.rsqrt(spread + EPS) * scale + shift).astype(jnp.bfloat16)


def project_qkv(normed_ref, w_ref, qkv_ref):
    normed = normed_ref[...]
    for part in range(3):
        start = part * SECTION
        qkv_ref[:, start + SECTION - 128 : start + SECTION] = jnp.zeros((normed.shape[0], 128), jnp.bfloat16)
    rows = normed.shape[0] // 2
    for at in range(0, 2 * rows, rows):
        full = lax.dot_general(normed[at : at + rows], w_ref[...], NT, preferred_element_type=jnp.float32)
        for part in range(3):
            qkv_ref[at : at + rows, part * SECTION : part * SECTION + HD] = full[
                :, part * HD : (part + 1) * HD
            ].astype(jnp.bfloat16)


def attend(groups, group_of, qkv_ref, s_ref, p_ref, mix_ref):
    factor = math.log2(math.e) / math.sqrt(HEAD_DIM)
    lane = lax.broadcasted_iota(jnp.int32, (1, 256), 1)
    tasks = [(h, start, size) for start, size in groups for h in range(HEADS)]

    def window(h):
        base = (HEAD_DIM * h) // 128 * 128
        low = HEAD_DIM * h - base
        return base, (lane >= low) & (lane < low + HEAD_DIM)

    def scores(t):
        h, start, size = tasks[t]
        base, own = window(h)
        rows = pl.ds(start, size)
        q = jnp.where(own, qkv_ref[rows, pl.ds(base, 256)], jnp.bfloat16(0))
        k = qkv_ref[rows, pl.ds(SECTION + base, 256)]
        s_ref[t % 2, :size, :size] = lax.dot_general(q, k, NT, preferred_element_type=jnp.float32)

    def weights(t):
        h, start, size = tasks[t]
        same = group_of(lax.broadcasted_iota(jnp.int32, (size, 1), 0)) == group_of(
            lax.broadcasted_iota(jnp.int32, (1, size), 1)
        )
        s = jnp.where(same, s_ref[t % 2, :size, :size], LOW)
        raised = jnp.exp2((s - jnp.max(s, axis=-1, keepdims=True)) * factor)
        inverse = 1.0 / jnp.sum(raised, axis=-1, keepdims=True)
        p_ref[t % 2, :size, :size] = (raised * inverse).astype(jnp.bfloat16)

    def mixing(t):
        h, start, size = tasks[t]
        base, own = window(h)
        rows = pl.ds(start, size)
        mixed = jnp.dot(
            p_ref[t % 2, :size, :size],
            qkv_ref[rows, pl.ds(2 * SECTION + base, 256)],
            preferred_element_type=jnp.float32,
        ).astype(jnp.bfloat16)
        mix_ref[rows, pl.ds(base, 256)] = jnp.where(own, mixed, mix_ref[rows, pl.ds(base, 256)])

    scores(0)
    for t in range(len(tasks)):
        if t + 1 < len(tasks):
            scores(t + 1)
        weights(t)
        mixing(t)


def sent(refs):
    far = refs[2:]
    return [refs[0]] + [ref.at[0] for ref in far] + [refs[1]] + [ref.at[1] for ref in far]


def sent_shapes(rows, width, dtype):
    near, far = jax.ShapeDtypeStruct((rows, width), dtype), jax.ShapeDtypeStruct((2, rows, width), dtype)
    return [near] * 2 + [far] * (CHIPS - 1)


def arrived(refs):
    crossed, near, moved = refs[:CHIPS], refs[CHIPS], refs[CHIPS + 1 :]
    parts = {0: near, CHIPS: crossed[0]}
    for place, d in enumerate(ARRIVAL):
        parts[d] = moved[place].at[0]
        parts[CHIPS + d] = crossed[1 + place]
    return [parts[part] for part in range(2 * CHIPS)]


def spatial_kernel(
    groups, group_of, place_ref, x_ref, mod_ref, w_ref, wo_ref, *refs
):
    o_ref, frames_ref, normed_ref, qkv_ref, s_ref, p_ref, mix_ref = refs
    frame_count = x_ref.shape[1]
    patches = frames_ref.shape[0] // frame_count

    def load(at, step):
        k, w = at // patches, at % patches // 2
        rows = x_ref[w : w + step // 2, k].reshape(step, x_ref.shape[3])
        frames_ref[at : at + step] = rows
        return rows

    normalize(load, mod_ref, 0, normed_ref)
    project_qkv(normed_ref, w_ref, qkv_ref)
    mix_ref[...] = jnp.zeros_like(mix_ref)
    attend(groups, group_of, qkv_ref, s_ref, p_ref, mix_ref)
    shards = 2 * CHIPS
    chips = [(d - place_ref[0]) & (CHIPS - 1) for d in range(CHIPS)]
    cores = [place_ref[1], 1 - place_ref[1]]
    widest = patches // shards
    for start, size in groups:
        rows = pl.ds(start, size)
        projected = jnp.dot(mix_ref[rows, 0:HD], wo_ref[...], preferred_element_type=jnp.float32)
        after = (frames_ref[rows, :].astype(jnp.float32) + mod_ref[2:3, :] * projected).astype(jnp.bfloat16)
        for at in range(0, size, widest):
            k, j = (start + at) // patches, (start + at) % patches // widest
            o_ref[chips[j // 2], cores[j % 2], k * widest : (k + 1) * widest, :] = after[at : at + widest]


def spatial_block(place, gathered, mod, w_qkv, w_out, groups, group_of, shards):
    pieces, frame_count, piece, width = gathered.shape
    rows = pieces * frame_count * piece
    biggest = max(size for _, size in groups)
    return pl.pallas_call(
        functools.partial(spatial_kernel, groups, group_of),
        out_shape=jax.ShapeDtypeStruct((CHIPS, 2, rows // shards, width), gathered.dtype),
        in_specs=[SMEM] + [VMEM] * 4,
        out_specs=VMEM,
        scratch_shapes=[
            pltpu.VMEM((rows, width), jnp.bfloat16),
            pltpu.VMEM((rows, width), jnp.bfloat16),
            pltpu.VMEM((rows, 3 * SECTION), jnp.bfloat16),
            pltpu.VMEM((2, biggest, biggest), jnp.float32),
            pltpu.VMEM((2, biggest, biggest), jnp.bfloat16),
            pltpu.VMEM((rows, SECTION), jnp.bfloat16),
        ],
        compiler_params=limit(28),
    )(place, gathered, mod, w_qkv, w_out)


def regroup(first, second):
    low = lax.broadcasted_iota(jnp.int32, (8, 1), 0) < 4
    return (
        jnp.where(low, first, pltpu.roll(second, 4, 0)),
        jnp.where(low, pltpu.roll(first, 4, 0), second),
    )


def temporal_kernel(groups, group_of, mod_ref, w_ref, *refs):
    parts = 2 * CHIPS
    incoming, outgoing = arrived(refs[:parts]), sent(refs[parts : parts + CHIPS + 1])
    normed_ref, qkv_ref, s_ref, p_ref, mix_ref = refs[parts + CHIPS + 1 :]
    runs = refs[0].shape[0] // 8
    half = normed_ref.shape[0] // 2
    scale = 1.0 + mod_ref[4:5, :]
    shift = mod_ref[3:4, :]

    def run(place):
        return incoming[place // runs][place % runs * 8 : place % runs * 8 + 8]

    for at in range(0, half, 8):
        values = jnp.concatenate([run(at // 4), run(at // 4 + 1)], axis=0).astype(jnp.float32)
        center = values - jnp.mean(values, axis=-1, keepdims=True)
        spread = jnp.mean(center * center, axis=-1, keepdims=True)
        normed = center * lax.rsqrt(spread + EPS) * scale + shift
        for start, rows in zip((at, half + at), regroup(normed[:8], normed[8:])):
            normed_ref[start : start + 8] = rows.astype(jnp.bfloat16)
    project_qkv(normed_ref, w_ref, qkv_ref)
    mix_ref[...] = jnp.zeros_like(mix_ref)
    attend(groups, group_of, qkv_ref, s_ref, p_ref, mix_ref)
    for at in range(0, half, 8):
        low = mix_ref[at : at + 8, 0:HD].astype(jnp.float32)
        high = mix_ref[half + at : half + at + 8, 0:HD].astype(jnp.float32)
        for place, rows in zip((at // 4, at // 4 + 1), regroup(low, high)):
            b, start = place // runs, place % runs * 8
            outgoing[b // CHIPS * CHIPS + -b % CHIPS][start : start + 8] = rows.astype(jnp.bfloat16)


def temporal_block(parts, mod, w_qkv, groups, group_of):
    rows, width = parts[0].shape
    total = rows * len(parts)
    biggest = max(size for _, size in groups)
    return pl.pallas_call(
        functools.partial(temporal_kernel, groups, group_of),
        out_shape=sent_shapes(rows, HD, parts[0].dtype),
        in_specs=[VMEM] * (2 + len(parts)),
        out_specs=[VMEM] * (CHIPS + 1),
        scratch_shapes=[
            pltpu.VMEM((total, width), jnp.bfloat16),
            pltpu.VMEM((total, 3 * SECTION), jnp.bfloat16),
            pltpu.VMEM((2, biggest, biggest), jnp.float32),
            pltpu.VMEM((2, biggest, biggest), jnp.bfloat16),
            pltpu.VMEM((total, SECTION), jnp.bfloat16),
        ],
        compiler_params=limit(28),
    )(mod, w_qkv, *parts)


def final_kernel(place_ref, mod_ref, wo_ref, after_ref, *refs):
    parts = 2 * CHIPS
    mixed_refs = arrived(refs[:parts])
    o_hbm, all_ref, out_ref, sems = refs[parts:]
    rows = after_ref.shape[2]
    frame_count, widest = o_hbm.shape[0], o_hbm.shape[2]
    stores = []
    for half in range(2):
        for d in range(CHIPS):
            all_ref[half, d * rows : (d + 1) * rows] = mixed_refs[half * CHIPS + -d % CHIPS][...]
        projected = jnp.dot(all_ref[half], wo_ref[...], preferred_element_type=jnp.float32)
        core = place_ref[1] if half == 0 else 1 - place_ref[1]
        for d in range(CHIPS):
            part = half * CHIPS + d
            after = after_ref[d, half].astype(jnp.float32)
            result = (after + mod_ref[5:6, :] * projected[d * rows : (d + 1) * rows]).astype(jnp.bfloat16)
            for k in range(frame_count):
                out_ref[part, k] = result[k * widest : (k + 1) * widest]
            j = 2 * ((place_ref[0] + d) & (CHIPS - 1)) + core
            stores.append(pltpu.make_async_copy(out_ref.at[part], o_hbm.at[:, j], sems.at[part]))
            stores[-1].start()
    for store in stores:
        store.wait()


def final_block(place, mixed, after, mod, w_out):
    rows, width = after.shape[2:]
    parts = len(mixed)
    return pl.pallas_call(
        final_kernel,
        out_shape=jax.ShapeDtypeStruct((NFD, parts, rows // NFD, width), after.dtype),
        in_specs=[SMEM] + [VMEM] * (3 + parts),
        out_specs=ANY,
        scratch_shapes=[
            pltpu.VMEM((2, CHIPS * rows, HD), jnp.bfloat16),
            pltpu.VMEM((parts, NFD, rows // NFD, width), jnp.bfloat16),
            pltpu.SemaphoreType.DMA((parts,)),
        ],
        compiler_params=limit(26),
    )(place, mod, w_out, after, *mixed)


def exchange(near, crossing, *far):
    places = range(2 * CHIPS)

    def cross(part):
        return lax.ppermute(part, "seq", [(i, i ^ 1) for i in places])

    moved = [
        lax.ppermute(far[d - 1], "seq", [(i, (i // 2 + d) % CHIPS * 2 + i % 2) for i in places])
        for d in ARRIVAL
    ]
    return [cross(crossing), *(cross(part[1]) for part in moved), near, *moved]


def source_index(counts, dest):
    groups, slots = dest.shape
    slot_ids = jnp.arange(slots, dtype=jnp.int32)
    live = slot_ids[None, :] < counts[:, None]
    targets = jnp.where(live, dest, -1).reshape(-1)
    wanted = jnp.arange(groups * NFD, dtype=jnp.int32)
    anchors = jnp.arange(groups * slots, dtype=jnp.int32)
    return jnp.sum(jnp.where(targets[None, :] == wanted[:, None], anchors[None, :], 0), axis=1)


def on_device(slot_tokens, modulation, counts, dest, qkv_spatial, out_spatial, qkv_temporal, out_temporal):
    groups = lax.axis_size("dp")
    shards = lax.axis_size("seq")
    slots, patches, width = slot_tokens.shape
    piece = patches // groups
    spread = lax.all_to_all(spread_pieces(slot_tokens, groups), "dp", split_axis=0, concat_axis=0, tiled=True)
    place = (lax.axis_index("seq") >> jnp.array([1, 0], jnp.int32)) & jnp.array([CHIPS - 1, 1], jnp.int32)
    spread, mod, index, place = lax.optimization_barrier(
        (spread, modulation[0], source_index(counts, dest), place)
    )
    chosen = choose_pieces(spread.reshape(groups * slots, piece, width), index)
    gathered = lax.all_to_all(
        chosen.reshape(groups, NFD, piece, width), "dp", split_axis=0, concat_axis=0, tiled=True
    )
    shift = patches.bit_length() - 1
    after = spatial_block(
        place,
        gathered,
        mod,
        qkv_spatial.T,
        out_spatial,
        ((0, 4 * patches), (4 * patches, 3 * patches)),
        lambda row: row >> shift,
        shards,
    )
    widest = patches // shards
    mixed = temporal_block(
        exchange(after[0, 0], after[0, 1], *(after[d] for d in range(1, CHIPS))),
        mod,
        qkv_temporal.T,
        ((0, NFD * patches // 2), (NFD * patches // 2, NFD * patches // 2)),
        lambda row: row & (widest // 2 - 1),
    )
    return final_block(place, exchange(*mixed), after, mod, out_temporal).reshape(NFD, patches, width)


def solution(mesh):
    in_specs = (P("dp", "seq", None), P("dp", None, None), P(), P(), P(), P(), P(), P())
    return jax.shard_map(
        on_device, mesh=mesh, in_specs=in_specs, out_specs=P("dp", "seq", None), check_vma=False
    )
```
